32 devices in a mesh: dp: 8 (over y, x, core), tensor: 4 (over z).
Axes of the slice: x: 2, y: 2, z: 4, core: 2. Of those that a mesh axis runs over, the one named last changes fastest.
Arguments:
- tokens: bfloat16 [8192, 1536], P('dp'), may hold values from -6 to 6
- teacher_feats: bfloat16 [8192, 256], P('dp'), may hold values from -12 to 12
- masks: int32 [32, 256], P('dp'), may hold values from 0 to 1, as said below
- w_in: bfloat16 [1536, 2048], P('dp'), may hold values from -0.15625 to 0.15625
- w_out: bfloat16 [2048, 256], P('dp'), may hold values from -0.125 to 0.125
- proto_student: bfloat16 [256, 131072], P(None, ('dp', 'tensor')), may hold values from -0.375 to 0.375
- proto_teacher: bfloat16 [256, 131072], P(None, ('dp', 'tensor')), may hold values from -1 to 1
Outputs:
- d_tokens: bfloat16 [8192, 1536], P('dp')
- grad_in: float32 [1536, 2048], P('dp')
- grad_out: float32 [2048, 256], P('dp')
- grad_proto: float32 [256, 131072], P(None, ('dp', 'tensor'))
- crop_loss: float32 [32], P('dp')
The draws below stay inside these ranges and needn't reach their ends.
Inputs may be any that keep to these rules, and one draw needn't show every extreme that they name: `masks`: the crops of one index of dp hold 256 or fewer masked patches together, exactly 256 on some index; a crop holds at most 129.
All inputs are finite; a program needn't handle non-finite values.
Results may differ from the reference program's by a relative error of at most 0.02.
Values may be sent and summed in bfloat16 or wider, within the bound.
A program may use at most 192 MiB of HBM per device.

```python
import math
import jax
import jax.numpy as jnp
from jax import lax

D = 1536
HID = 2048
BOT = 256
PROTOS = 131072
PATCHES = 256
ROUNDS = 3
CROPS_DEV = 4
CAP = 256
CROPS = 32
N_DP = 8
N_TENSOR = 4


def draw_masks(key, part):
    crops = CROPS_DEV * N_DP
    base_key = jax.random.fold_in(key, 4241)
    key_total, key_full, key_move, key_perm = jax.random.split(base_key, 4)
    totals = jax.random.randint(key_total, (N_DP,), CAP // 4, CAP + 1)
    fullest = jax.random.randint(key_full, (), 0, N_DP)
    totals = jnp.where(jnp.arange(N_DP) == fullest, CAP, totals)
    base = totals // CROPS_DEV
    extra = totals % CROPS_DEV
    counts = base[:, None] + (jnp.arange(CROPS_DEV)[None, :] < extra[:, None]).astype(jnp.int32)
    pairs = counts.reshape(N_DP, CROPS_DEV // 2, 2)
    moved = jax.random.randint(key_move, (N_DP, CROPS_DEV // 2), 0, base[:, None] + 1)
    pairs = pairs + jnp.stack([moved, -moved], axis=-1)
    counts = pairs.reshape(crops)
    orders = jax.vmap(lambda sub: jax.random.permutation(sub, PATCHES))(jax.random.split(key_perm, crops))
    return (orders < counts[:, None]).astype(jnp.int32)


def cluster_layout(key, spread):
    cluster_total = 24
    base_key = jax.random.fold_in(key, 7001)
    key_dir, key_rows, key_cols = jax.random.split(base_key, 3)
    centres = jax.random.normal(key_dir, (cluster_total, BOT), jnp.float32)
    centres = centres / jnp.sqrt(jnp.sum(centres * centres, axis=1, keepdims=True))
    ladder = jnp.arange(cluster_total).astype(jnp.float32) / (cluster_total - 1.0)
    row_logits = spread * jnp.take(ladder, jax.random.permutation(key_rows, cluster_total))
    col_logits = spread * jnp.take(ladder, jax.random.permutation(key_cols, cluster_total))
    return (centres, row_logits, col_logits)


def draw_teacher_feats(key, part):
    patch_total = CROPS_DEV * N_DP * PATCHES
    spread = math.log(10.0)
    centres, row_logits, col_logits = cluster_layout(key, spread)
    own_key = jax.random.fold_in(key, 7103)
    key_pick, key_noise = jax.random.split(own_key, 2)
    chosen = jax.random.categorical(key_pick, row_logits, shape=(patch_total,))
    root_bot = math.sqrt(BOT)
    noise = jax.random.normal(key_noise, (patch_total, BOT), jnp.float32)
    values = jnp.take(centres, chosen, axis=0) * root_bot + 1.1 * noise
    return jnp.clip(values, -12.0, 12.0).astype(jnp.bfloat16)


def draw_proto_teacher(key, part):
    spread = math.log(10.0)
    centres, row_logits, col_logits = cluster_layout(key, spread)
    own_key = jax.random.fold_in(key, 7207)
    key_pick, key_noise = jax.random.split(own_key, 2)
    shard_cols = PROTOS // (N_DP * N_TENSOR)
    owner = jnp.arange(PROTOS) // shard_cols % N_TENSOR
    tied = (jnp.arange(24)[None, :] % N_TENSOR == owner[:, None]).astype(jnp.float32)
    logits = col_logits[None, :] + 4.0 * tied
    chosen = jax.random.categorical(key_pick, logits, axis=1)
    root_bot = math.sqrt(BOT)
    noise = jax.random.normal(key_noise, (BOT, PROTOS), jnp.float32)
    values = (jnp.take(centres, chosen, axis=0).T * root_bot + 1.1 * noise) / root_bot
    return jnp.clip(values, -1.0, 1.0).astype(jnp.bfloat16)


def spiked(drawn, key, source, target, blocks, factor):
    owner, partner = [(jnp.arange(drawn.shape[axis_at]) // (drawn.shape[axis_at] // blocks)).reshape([-1 if axis == axis_at else 1 for axis in range(drawn.ndim)]) for axis_at in (source, target)]
    chosen = jax.random.permutation(key, blocks)[partner]
    strong = (owner == chosen) | (owner == (partner + blocks // 2) % blocks)
    return jnp.where(strong, factor * drawn, drawn)


def block_scale(stream_key, shape, cuts, least, top_value):
    def one(position, blocks):
        steps = jax.random.uniform(jax.random.fold_in(jax.random.fold_in(stream_key, 6), position), (blocks,), jnp.float32, least / len(cuts), top_value / len(cuts))
        return jnp.repeat(jnp.exp(steps), shape[position] // blocks).reshape((-1,) + (1,) * (len(shape) - position - 1))

    gain = one(*cuts[0])
    for cut in cuts[1:]:
        gain = gain * one(*cut)
    return gain


def gaussian(key, extent, scale, bound, cuts=(), dtype=jnp.bfloat16):
    values = jax.random.normal(key, extent, jnp.float32) * scale
    if len(cuts) > 0:
        values = block_scale(key, extent, cuts, -0.22, 0.18) * values
    return jnp.clip(values, min=-bound, max=bound).astype(dtype)


def noise_with(stream_key, shape, deviation, reach, cuts, heavy, held_as=jnp.bfloat16):
    result = deviation * jax.random.normal(stream_key, shape, jnp.float32)
    if cuts:
        result = result * block_scale(stream_key, shape, cuts, -0.22, 0.18)
    return jnp.clip(spiked(result, jax.random.fold_in(stream_key, 3), *heavy), -reach, reach).astype(held_as)


def setup_inputs(seed: int = 0) -> dict:
    streams_of = jax.random.split(jax.random.key(seed), 8)
    return {
        "tokens": noise_with(streams_of[0], (CROPS * PATCHES, D), 1.0, 6.0, ((0, 8),), (0, 1, 8, 2.0)),
        "teacher_feats": draw_teacher_feats(jax.random.fold_in(streams_of[7], 71), 0),
        "masks": draw_masks(jax.random.fold_in(streams_of[7], 71), 0),
        "w_in": gaussian(streams_of[3], (D, HID), D ** -0.5, 0.15625, ((0, 8),)),
        "w_out": gaussian(streams_of[4], (HID, BOT), HID ** -0.5, 0.125, ((0, 8),)),
        "proto_student": gaussian(streams_of[5], (BOT, PROTOS), BOT ** -0.5, 0.375, ((1, 32),)),
        "proto_teacher": draw_proto_teacher(jax.random.fold_in(streams_of[7], 71), 0),
    }


TEACHER_TEMP = 0.07
STUDENT_TEMP = 0.1
EPS = 1e-06
GRAD_SCALE = 65536.0

def gelu_parts(pre):
    cdf = 0.5 * (1.0 + lax.erf(pre * 0.7071067811865476))
    pdf = jnp.exp(-0.5 * pre * pre) * 0.3989422804014327
    return (pre * cdf, cdf + pre * pdf)

def unit_rows(feats):
    inverse = lax.rsqrt(lax.optimization_barrier(jnp.sum(feats * feats, axis=1, keepdims=True)) + EPS)
    return (feats * inverse, inverse)

def unit_columns(protos):
    wide = protos.astype(jnp.float32)
    norms = jnp.sqrt(lax.optimization_barrier(jnp.sum(wide * wide, axis=0, keepdims=True)) + EPS)
    return (wide / norms, norms)

def matmul(left, right):
    return jnp.dot(left.astype(jnp.float32), right.astype(jnp.float32), precision=lax.Precision.HIGHEST)

def rounded(value):
    return lax.optimization_barrier(value.astype(jnp.bfloat16)).astype(jnp.float32)

def reference(tokens, teacher_feats, masks, w_in, w_out, proto_student, proto_teacher):
    groups = N_DP
    per_dev = CROPS_DEV * PATCHES
    total = groups * CAP
    flat = masks.reshape(groups, per_dev)

    def pick(bits):
        return jnp.nonzero(bits, size=CAP, fill_value=0)[0].astype(jnp.int32)
    index = jax.vmap(pick)(flat)
    count = lax.optimization_barrier(jnp.sum(flat, axis=1))
    livef = (jnp.arange(CAP)[None, :] < count[:, None]).astype(jnp.float32)
    crop_count = lax.optimization_barrier(jnp.sum(masks, axis=1)).reshape(groups, CROPS_DEV)
    inverse = 1.0 / jnp.maximum(crop_count, 1).astype(jnp.float32)
    member = (index[:, :, None] // PATCHES == jnp.arange(CROPS_DEV)[None, None, :]).astype(jnp.float32) * livef[:, :, None]
    weight = (GRAD_SCALE * lax.optimization_barrier(jnp.sum(member * inverse[:, None, :], axis=2))).astype(jnp.bfloat16)

    def take_rows(table, idx):
        return table[idx]
    rows = jax.vmap(take_rows)(tokens.reshape(groups, per_dev, D), index).reshape(total, D)
    teacher_pick = jax.vmap(take_rows)(teacher_feats.reshape(groups, per_dev, BOT), index).reshape(total, BOT)
    live_all = livef.reshape(total)
    weight_all = weight.reshape(total).astype(jnp.float32)
    pre = matmul(rows, w_in)
    act, slope = gelu_parts(pre)
    hidden = act.astype(jnp.bfloat16)
    feats = matmul(hidden, w_out)
    unit, inv = unit_rows(feats)
    student_rows = unit.astype(jnp.bfloat16).astype(jnp.float32)
    teacher_rows = unit_rows(teacher_pick.astype(jnp.float32))[0].astype(jnp.bfloat16).astype(jnp.float32)
    s_cols, s_norm = unit_columns(proto_student)
    t_cols, _ = unit_columns(proto_teacher)
    width = min(8192, PROTOS)
    count_blocks = PROTOS // width

    def blocks(matrix):
        return matrix.reshape(BOT, count_blocks, width).transpose(1, 0, 2)
    s_blocks = blocks(s_cols.astype(jnp.bfloat16).astype(jnp.float32))
    t_blocks = blocks(t_cols.astype(jnp.bfloat16).astype(jnp.float32))

    def teacher_exp(tcol):
        return jnp.exp(matmul(teacher_rows, tcol) / TEACHER_TEMP) * live_all[:, None]
    scale_row = live_all
    for turn in range(ROUNDS - 1):

        def step(acc, tcol):
            expo = teacher_exp(tcol)
            col_scale = 1.0 / lax.optimization_barrier(jnp.sum(expo * scale_row[:, None], axis=0))
            return (acc + lax.optimization_barrier(jnp.sum(expo * col_scale[None, :], axis=1)), col_scale)
        row_sum, _ = lax.scan(step, jnp.zeros((total,), jnp.float32), t_blocks)
        scale_row = live_all / (row_sum + 1.0 - live_all)

    def last_step(acc, both):
        tcol, scol = both
        expo = teacher_exp(tcol)
        col_scale = 1.0 / lax.optimization_barrier(jnp.sum(expo * scale_row[:, None], axis=0))
        balanced = expo * col_scale[None, :]
        scores = matmul(student_rows, scol) / STUDENT_TEMP
        acc = (acc[0] + lax.optimization_barrier(jnp.sum(balanced, axis=1)), acc[1] + lax.optimization_barrier(jnp.sum(jnp.exp(scores), axis=1)), acc[2] + lax.optimization_barrier(jnp.sum(balanced * scores, axis=1)))
        return (acc, col_scale)
    zero = jnp.zeros((total,), jnp.float32)
    (row_sum, norm_sum, cross), col_last = lax.scan(last_step, (zero, zero, zero), (t_blocks, s_blocks))
    scale_last = live_all / (row_sum + 1.0 - live_all)
    row_loss = jnp.log(norm_sum) - scale_last * cross
    crop_loss = (lax.optimization_barrier(jnp.sum(member * row_loss.reshape(groups, CAP)[:, :, None], axis=1)) * inverse).reshape(groups * CROPS_DEV)

    def back_step(grad_acc, three):
        tcol, scol, col_scale = three
        expo = teacher_exp(tcol)
        balanced = expo * col_scale[None, :]
        target = balanced * scale_last[:, None]
        scores = matmul(student_rows, scol) / STUDENT_TEMP
        probs = jnp.exp(scores) / norm_sum[:, None]
        grad_score = (weight_all[:, None] * (probs - target) / STUDENT_TEMP).astype(jnp.bfloat16).astype(jnp.float32)
        grad_acc = grad_acc + matmul(grad_score, scol.T)
        parts = jnp.einsum('grb,grk->gbk', student_rows.reshape(groups, CAP, BOT), grad_score.reshape(groups, CAP, width), precision=lax.Precision.HIGHEST)
        return (grad_acc, lax.optimization_barrier(jnp.sum(rounded(parts), axis=0)))
    grad_unit, grad_blocks = lax.scan(back_step, jnp.zeros((total, BOT), jnp.float32), (t_blocks, s_blocks, col_last))
    grad_cols = grad_blocks.transpose(1, 0, 2).reshape(BOT, PROTOS)
    grad_proto = (grad_cols - s_cols * lax.optimization_barrier(jnp.sum(s_cols * grad_cols, axis=0, keepdims=True))) / s_norm
    inner = lax.optimization_barrier(jnp.sum(unit * grad_unit, axis=1, keepdims=True))
    grad_feats = (inv * (grad_unit - unit * inner)).astype(jnp.bfloat16).astype(jnp.float32)
    hidden_wide = hidden.astype(jnp.float32)
    out_parts = jnp.einsum('grh,grb->ghb', hidden_wide.reshape(groups, CAP, HID), grad_feats.reshape(groups, CAP, BOT), precision=lax.Precision.HIGHEST)
    grad_out = lax.optimization_barrier(jnp.sum(rounded(out_parts), axis=0))
    grad_pre = (matmul(grad_feats, w_out.T) * slope).astype(jnp.bfloat16).astype(jnp.float32)
    in_parts = jnp.einsum('grd,grh->gdh', rows.astype(jnp.float32).reshape(groups, CAP, D), grad_pre.reshape(groups, CAP, HID), precision=lax.Precision.HIGHEST)
    grad_in = lax.optimization_barrier(jnp.sum(rounded(in_parts), axis=0))
    grad_rows = (matmul(grad_pre, w_in.T) * live_all[:, None]).reshape(groups, CAP, D)

    def place(idx, values):
        return jnp.zeros((per_dev, D), jnp.float32).at[idx].add(values)
    d_tokens = jax.vmap(place)(index, grad_rows).reshape(groups * per_dev, D).astype(jnp.bfloat16)
    return (d_tokens, grad_in, grad_out, grad_proto, crop_loss)
```

```python
import functools

import jax
import jax.numpy as jnp
from jax import lax
from jax.experimental import pallas as pl
from jax.experimental.pallas import tpu as pltpu
from jax.sharding import PartitionSpec as P

ROUNDS = 3
CAP = 256

TEACHER_TEMP = 0.07
STUDENT_TEMP = 0.1
EPS = 1e-06
GRAD_SCALE = 65536.0
LANES = 128
BLOCK = 512
MESH = pl.DeviceIdType.MESH
F32 = jnp.float32
BF16 = jnp.bfloat16


def gelu_parts(pre):
    cdf = 0.5 * (1.0 + lax.erf(pre * 0.7071067811865476))
    pdf = jnp.exp(-0.5 * pre * pre) * 0.3989422804014327
    return (pre * cdf, cdf + pre * pdf)


def unit_rows(feats):
    inverse = lax.rsqrt(jnp.sum(feats * feats, axis=1, keepdims=True) + EPS)
    return (feats * inverse, inverse)


def unit_columns(protos):
    wide = protos.astype(F32)
    norms = jnp.sqrt(jnp.sum(wide * wide, axis=0, keepdims=True) + EPS)
    return (wide / norms, norms)


def spread(dense, out_ref):
    for c in range(dense.shape[0]):
        row = jnp.broadcast_to(dense[c : c + 1, :], (LANES, LANES))
        out_ref[c * LANES : (c + 1) * LANES, :] = row.T


def gathered(acc_ref, out_ref, base):
    for c in range(acc_ref.shape[0] // LANES):
        turned = acc_ref[c * LANES : (c + 1) * LANES, :].T
        out_ref[base + c : base + c + 1, :] = jnp.sum(turned, axis=0, keepdims=True)


def fold_rows(values):
    rows, cols = values.shape
    return jnp.sum(values.reshape(rows // 8, 8, cols), axis=0)


def fold_lanes(values):
    total = values[:, :LANES]
    for start in range(LANES, values.shape[1], LANES):
        total = total + values[:, start : start + LANES]
    return total


def widen(values, cols):
    return jnp.concatenate([values] * (cols // LANES), axis=1)


def chunk(step):
    return pl.ds(pl.multiple_of(step * CAP, CAP), CAP)


def first_kernel(teach, proto, live, expo, sums, live_b, acc):
    rows, block = expo.shape
    here = pl.program_id(0)

    @pl.when(here == 0)
    def _():
        spread(live[...], live_b)
        acc[...] = jnp.zeros_like(acc)

    cols = unit_columns(proto[...])[0].astype(BF16)

    def raise_rows(step, total):
        part = chunk(step)
        cos = jnp.dot(teach[part, :], cols, preferred_element_type=F32)
        value = (jnp.exp(cos * (1.0 / TEACHER_TEMP)) * widen(live_b[part, :], block)).astype(BF16)
        expo[part, :] = value
        return total + fold_rows(value.astype(F32))

    total = lax.fori_loop(0, rows // CAP, raise_rows, jnp.zeros((8, block), F32))
    scale = 1.0 / jnp.sum(total, axis=0, keepdims=True)

    def sum_rows(step, carry):
        part = chunk(step)
        acc[part, :] += fold_lanes(expo[part, :].astype(F32) * scale)
        return carry

    lax.fori_loop(0, rows // CAP, sum_rows, 0)

    @pl.when(here == pl.num_programs(0) - 1)
    def _():
        gathered(acc, sums, 0)


def row_scale(live, row_sum):
    return live / (row_sum + 1.0 - live)


def column_scale(expo, u_b):
    rows, block = expo.shape

    def step_total(step, total):
        part = chunk(step)
        return total + fold_rows(expo[part, :].astype(F32) * widen(u_b[part, :], block))

    total = lax.fori_loop(0, rows // CAP, step_total, jnp.zeros((8, block), F32))
    return 1.0 / jnp.sum(total, axis=0, keepdims=True)


def middle_kernel(expo, live, row_sum, sums, u_b, acc):
    rows, block = expo.shape
    here = pl.program_id(0)

    @pl.when(here == 0)
    def _():
        spread(row_scale(live[...], row_sum[...]), u_b)
        acc[...] = jnp.zeros_like(acc)

    scale = column_scale(expo, u_b)

    def sum_rows(step, carry):
        part = chunk(step)
        acc[part, :] += fold_lanes(expo[part, :].astype(F32) * scale)
        return carry

    lax.fori_loop(0, rows // CAP, sum_rows, 0)

    @pl.when(here == pl.num_programs(0) - 1)
    def _():
        gathered(acc, sums, 0)


def last_kernel(expo, live, row_sum, student, proto, raised, v_out, sums, u_b, acc, acc_n, acc_c):
    rows, block = expo.shape
    here = pl.program_id(0)

    @pl.when(here == 0)
    def _():
        spread(row_scale(live[...], row_sum[...]), u_b)
        acc[...] = jnp.zeros_like(acc)
        acc_n[...] = jnp.zeros_like(acc_n)
        acc_c[...] = jnp.zeros_like(acc_c)

    scale = column_scale(expo, u_b)
    v_out[...] = jnp.broadcast_to(scale, v_out.shape)
    cols = unit_columns(proto[...])[0].astype(BF16)

    def sum_rows(step, carry):
        part = chunk(step)
        scores = jnp.dot(student[part, :], cols, preferred_element_type=F32) * (1.0 / STUDENT_TEMP)
        power = jnp.exp(scores)
        raised[part, :] = power.astype(BF16)
        balanced = expo[part, :].astype(F32) * scale
        acc[part, :] += fold_lanes(balanced)
        acc_n[part, :] += fold_lanes(power)
        acc_c[part, :] += fold_lanes(balanced * scores)
        return carry

    lax.fori_loop(0, rows // CAP, sum_rows, 0)

    @pl.when(here == pl.num_programs(0) - 1)
    def _():
        dense = rows // LANES
        gathered(acc, sums, 0)
        gathered(acc_n, sums, dense)
        gathered(acc_c, sums, 2 * dense)


def grad_kernel(
    expo, raised, v_in, live, weight, sums, student_t, proto, part_out, grad_out, prob_b, target_b, total, cols_total
):
    rows, block = expo.shape
    here = pl.program_id(0)
    dense = rows // LANES

    @pl.when(here == 0)
    def _():
        factor = weight[...] * (1.0 / STUDENT_TEMP)
        spread(factor / sums[dense : 2 * dense, :], prob_b)
        spread(factor * row_scale(live[...], sums[:dense, :]), target_b)
        total[...] = jnp.zeros_like(total)

    unit, norms = unit_columns(proto[...])
    cols = unit.astype(BF16)
    scale = v_in[0:1, :]
    cols_total[...] = jnp.zeros_like(cols_total)

    def one_group(step, carry):
        part = chunk(step)
        target = expo[part, :].astype(F32) * scale * widen(target_b[part, :], block)
        probs = raised[part, :].astype(F32) * widen(prob_b[part, :], block)
        score = (probs - target).astype(BF16)
        total[part, :] += lax.dot_general(
            score, cols, (((1,), (1,)), ((), ())), preferred_element_type=F32
        )
        term = jnp.dot(student_t[:, part], score, preferred_element_type=F32)
        cols_total[...] += term.astype(BF16).astype(F32)
        return carry

    lax.fori_loop(0, rows // CAP, one_group, 0)
    grad = cols_total[...]
    grad_out[...] = (grad - unit * jnp.sum(unit * grad, axis=0, keepdims=True)) / norms

    @pl.when(here == pl.num_programs(0) - 1)
    def _():
        part_out[...] = total[...].astype(BF16)


def whole(shape):
    return pl.BlockSpec(shape, lambda i: tuple(0 for _ in shape))


def tall(rows, block):
    return pl.BlockSpec((rows, block), lambda i: (0, i))


def params(**extra):
    return pltpu.CompilerParams(
        dimension_semantics=("arbitrary",), vmem_limit_bytes=48 * 1024 * 1024, **extra
    )


def cost(flops, moved, powers):
    return pl.CostEstimate(flops=flops, bytes_accessed=moved, transcendentals=powers)


def prototype_first(teach, proto, live):
    rows, width = teach.shape
    columns = proto.shape[1]
    block = min(BLOCK, columns)
    return pl.pallas_call(
        first_kernel,
        name="first_round",
        grid=(columns // block,),
        in_specs=[whole(teach.shape), tall(width, block), whole(live.shape)],
        out_specs=[tall(rows, block), whole(live.shape)],
        out_shape=[jax.ShapeDtypeStruct((rows, columns), BF16), jax.ShapeDtypeStruct(live.shape, F32)],
        scratch_shapes=[pltpu.VMEM((rows, LANES), F32)] * 2,
        compiler_params=params(),
        cost_estimate=cost(2 * rows * width * columns, 2 * rows * columns, rows * columns),
    )(teach, proto, live)


def prototype_middle(expo, live, row_sum):
    rows, columns = expo.shape
    block = min(BLOCK, columns)
    return pl.pallas_call(
        middle_kernel,
        name="middle_round",
        grid=(columns // block,),
        in_specs=[tall(rows, block), whole(live.shape), whole(live.shape)],
        out_specs=whole(live.shape),
        out_shape=jax.ShapeDtypeStruct(live.shape, F32),
        scratch_shapes=[pltpu.VMEM((rows, LANES), F32)] * 2,
        compiler_params=params(),
        cost_estimate=cost(4 * rows * columns, 2 * rows * columns, 0),
    )(expo, live, row_sum)


def prototype_last(expo, live, row_sum, student, proto):
    rows, columns = expo.shape
    width = student.shape[1]
    block = min(BLOCK, columns)
    dense = live.shape[0]
    return pl.pallas_call(
        last_kernel,
        name="last_round",
        grid=(columns // block,),
        in_specs=[
            tall(rows, block),
            whole(live.shape),
            whole(live.shape),
            whole(student.shape),
            tall(width, block),
        ],
        out_specs=[tall(rows, block), tall(8, block), whole((3 * dense, LANES))],
        out_shape=[
            jax.ShapeDtypeStruct((rows, columns), BF16),
            jax.ShapeDtypeStruct((8, columns), F32),
            jax.ShapeDtypeStruct((3 * dense, LANES), F32),
        ],
        scratch_shapes=[pltpu.VMEM((rows, LANES), F32)] * 4,
        compiler_params=params(),
        cost_estimate=cost(2 * rows * width * columns, 4 * rows * columns, rows * columns),
    )(expo, live, row_sum, student, proto)


def prototype_grad(expo, raised, v, live, weight, sums, student_t, proto):
    rows, columns = expo.shape
    width = proto.shape[0]
    block = min(BLOCK, columns)
    return pl.pallas_call(
        grad_kernel,
        name="score_grad",
        grid=(columns // block,),
        in_specs=[
            tall(rows, block),
            tall(rows, block),
            tall(8, block),
            whole(live.shape),
            whole(live.shape),
            whole(sums.shape),
            whole(student_t.shape),
            tall(width, block),
        ],
        out_specs=[whole((rows, width)), tall(width, block)],
        out_shape=[
            jax.ShapeDtypeStruct((rows, width), BF16),
            jax.ShapeDtypeStruct((width, columns), F32),
        ],
        scratch_shapes=[pltpu.VMEM((rows, LANES), F32)] * 2
        + [pltpu.VMEM((rows, width), F32), pltpu.VMEM((width, block), F32)],
        compiler_params=params(),
        cost_estimate=cost(4 * rows * width * columns, 4 * rows * columns, 0),
    )(expo, raised, v, live, weight, sums, student_t, proto)


def greet(groups, many):
    barrier = pltpu.get_barrier_semaphore()
    for axis in ("dp", "tensor"):
        me = lax.axis_index(axis)
        for step in range(1, groups[axis]):
            peer = lax.rem(me + step, groups[axis])
            pl.semaphore_signal(barrier, inc=1, device_id={axis: peer}, device_id_type=MESH)
    pl.semaphore_wait(barrier, many)


def exchange(axis, n, source, landing, send, recv):
    me = lax.axis_index(axis)

    def copy(peer, slot):
        return pltpu.make_async_remote_copy(
            src_ref=source(peer),
            dst_ref=landing.at[slot],
            send_sem=send.at[peer],
            recv_sem=recv.at[slot],
            device_id={axis: peer},
            device_id_type=MESH,
        )

    for step in range(1, n):
        copy(lax.rem(me + step, n), me).start()
    for step in range(1, n):
        peer = lax.rem(me + step, n)
        copy(peer, peer).wait()


def total_kernel(groups, value, out, near, far, send_a, recv_a, send_b, recv_b):
    n, m = groups["dp"], groups["tensor"]
    greet(groups, n + m - 2)
    exchange("dp", n, lambda peer: value, near, send_a, recv_a)
    near[lax.axis_index("dp")] = value[...]
    part = near[0]
    for slot in range(1, n):
        part = part + near[slot]
    out[...] = part
    exchange("tensor", m, lambda peer: out, far, send_b, recv_b)
    far[lax.axis_index("tensor")] = part
    part = far[0]
    for slot in range(1, m):
        part = part + far[slot]
    out[...] = part


def everywhere_total(value, groups, ident):
    n, m = groups["dp"], groups["tensor"]
    return pl.pallas_call(
        functools.partial(total_kernel, groups),
        name=f"row_total_{ident}",
        in_specs=[pl.BlockSpec(memory_space=pltpu.VMEM)],
        out_specs=pl.BlockSpec(memory_space=pltpu.VMEM),
        out_shape=jax.ShapeDtypeStruct(value.shape, F32),
        scratch_shapes=[
            pltpu.VMEM((n,) + value.shape, F32),
            pltpu.VMEM((m,) + value.shape, F32),
            pltpu.SemaphoreType.DMA((n,)),
            pltpu.SemaphoreType.DMA((n,)),
            pltpu.SemaphoreType.DMA((m,)),
            pltpu.SemaphoreType.DMA((m,)),
        ],
        compiler_params=pltpu.CompilerParams(collective_id=ident, has_side_effects=True),
    )(value)


def owner_kernel(groups, value, out, near, far, part, send_a, recv_a, send_b, recv_b):
    n, m = groups["dp"], groups["tensor"]
    greet(groups, n + m - 2)
    me = lax.axis_index("dp")
    exchange("dp", n, lambda peer: value.at[peer], near, send_a, recv_a)
    near[me] = value[me]
    total = near[0].astype(F32)
    for slot in range(1, n):
        total = total + near[slot].astype(F32)
    part[...] = total.astype(BF16)
    exchange("tensor", m, lambda peer: part, far, send_b, recv_b)
    far[lax.axis_index("tensor")] = part[...]
    total = far[0].astype(F32)
    for slot in range(1, m):
        total = total + far[slot].astype(F32)
    out[...] = total


def owner_total(value, groups, ident):
    n, m = groups["dp"], groups["tensor"]
    own = value.shape[1:]
    return pl.pallas_call(
        functools.partial(owner_kernel, groups),
        name="owner_total",
        in_specs=[pl.BlockSpec(memory_space=pltpu.VMEM)],
        out_specs=pl.BlockSpec(memory_space=pltpu.VMEM),
        out_shape=jax.ShapeDtypeStruct(own, F32),
        scratch_shapes=[
            pltpu.VMEM((n,) + own, BF16),
            pltpu.VMEM((m,) + own, BF16),
            pltpu.VMEM(own, BF16),
            pltpu.SemaphoreType.DMA((n,)),
            pltpu.SemaphoreType.DMA((n,)),
            pltpu.SemaphoreType.DMA((m,)),
            pltpu.SemaphoreType.DMA((m,)),
        ],
        compiler_params=pltpu.CompilerParams(collective_id=ident, has_side_effects=True),
    )(value)


def head_forward(rows, w_in_all, w_out_all):
    pre = jnp.dot(rows, w_in_all, preferred_element_type=F32)
    act, slope = gelu_parts(pre)
    hidden = act.astype(BF16)
    feats = jnp.dot(hidden, w_out_all, preferred_element_type=F32)
    unit, inv = unit_rows(feats)
    return (hidden, slope, unit, inv, unit.astype(BF16))


def head_backward(rows, hidden, slope, unit, inv, grad_unit, w_in_all, w_out_all):
    inner = jnp.sum(unit * grad_unit, axis=1, keepdims=True)
    grad_feats = (inv * (grad_unit - unit * inner)).astype(BF16)
    grad_out_part = lax.dot_general(
        hidden, grad_feats, (((0,), (0,)), ((), ())), preferred_element_type=F32
    )
    grad_hidden = lax.dot_general(
        grad_feats, w_out_all, (((1,), (1,)), ((), ())), preferred_element_type=F32
    )
    grad_pre = (grad_hidden * slope).astype(BF16)
    grad_in_part = lax.dot_general(
        rows, grad_pre, (((0,), (0,)), ((), ())), preferred_element_type=F32
    )
    grad_rows = lax.dot_general(
        grad_pre, w_in_all, (((1,), (1,)), ((), ())), preferred_element_type=F32
    )
    return (grad_in_part, grad_out_part, grad_rows)


def selection(masks):
    crops, patches = masks.shape
    size = crops * patches
    flat = masks.reshape(1, size)
    before = (
        lax.broadcasted_iota(jnp.int32, (size, size), 0) < lax.broadcasted_iota(jnp.int32, (size, size), 1)
    ).astype(BF16)
    place = jnp.dot(flat.astype(BF16), before, preferred_element_type=F32).astype(jnp.int32)
    slots = lax.broadcasted_iota(jnp.int32, (CAP, size), 0)
    picked = (place == slots) & (flat > 0)
    dead = slots >= jnp.sum(flat)
    first = lax.broadcasted_iota(jnp.int32, (CAP, size), 1) == 0
    return (picked | (dead & first)).astype(BF16), picked.astype(BF16)


def shards(groups, tokens, teacher_feats, masks, w_in, w_out, proto_student, proto_teacher):
    w_in_all = lax.all_gather(w_in, "dp", axis=0, tiled=True)
    w_out_all = lax.all_gather(w_out, "dp", axis=0, tiled=True)
    pick, place = selection(masks)
    counts = jnp.sum(masks, axis=1)
    ends = jnp.sum(
        jnp.where(jnp.arange(counts.shape[0])[:, None] <= jnp.arange(counts.shape[0])[None, :], counts[:, None], 0),
        axis=0,
    )
    slot = jnp.arange(CAP)[:, None]
    member = ((slot >= (ends - counts)[None, :]) & (slot < ends[None, :])).astype(F32)
    inverse = 1.0 / jnp.maximum(counts, 1).astype(F32)
    weight = (GRAD_SCALE * jnp.sum(member * inverse[None, :], axis=1)).astype(BF16)
    teacher_pick = jnp.dot(pick, teacher_feats, preferred_element_type=F32)
    teacher_rows = unit_rows(teacher_pick)[0].astype(BF16)
    teacher_every = lax.all_gather(teacher_rows, "dp", axis=0, tiled=True)
    weight_every = lax.all_gather(weight, "dp", axis=0, tiled=True).astype(F32)
    weight_every = weight_every.reshape(-1, LANES)
    live_every = (weight_every > 0).astype(F32)

    expo, row_sum = prototype_first(teacher_every, proto_teacher, live_every)
    row_sum = everywhere_total(row_sum, groups, 1)

    rows = jnp.dot(pick, tokens, preferred_element_type=F32).astype(BF16)
    hidden, slope, unit, inv, student_rows = head_forward(rows, w_in_all, w_out_all)
    student_every = lax.all_gather(student_rows, "dp", axis=0, tiled=True)

    for turn in range(ROUNDS - 2):
        row_sum = prototype_middle(expo, live_every, row_sum)
        row_sum = everywhere_total(row_sum, groups, 2 + turn)
    raised, v, sums = prototype_last(expo, live_every, row_sum, student_every, proto_student)
    sums = everywhere_total(sums, groups, ROUNDS)
    grad_part, grad_proto = prototype_grad(
        expo, raised, v, live_every, weight_every, sums, student_every.T, proto_student
    )
    grad_unit = owner_total(grad_part.reshape(groups["dp"], CAP, -1), groups, ROUNDS + 1)

    dense = live_every.shape[0]
    own = CAP // LANES
    start = lax.axis_index("dp") * own

    def mine(values):
        return lax.dynamic_slice_in_dim(values, start, own).reshape(CAP)

    live_own = mine(live_every)
    scale_row = live_own / (mine(sums[:dense]) + 1.0 - live_own)
    row_loss = jnp.log(mine(sums[dense : 2 * dense])) - scale_row * mine(sums[2 * dense :])
    crop_loss = jnp.sum(member * row_loss[:, None], axis=0) * inverse

    grad_in_part, grad_out_part, grad_rows = head_backward(
        rows, hidden, slope, unit, inv, grad_unit, w_in_all, w_out_all
    )
    grad_in, grad_out = (
        lax.psum_scatter(grad_in_part.astype(BF16), "dp", scatter_dimension=0, tiled=True).astype(F32),
        lax.psum_scatter(grad_out_part.astype(BF16), "dp", scatter_dimension=0, tiled=True).astype(F32),
    )
    d_tokens = lax.dot_general(
        place, grad_rows.astype(BF16), (((0,), (0,)), ((), ())), preferred_element_type=F32
    ).astype(BF16)
    return (d_tokens, grad_in, grad_out, grad_proto, crop_loss)


def solution(mesh):
    groups = {"dp": mesh.shape["dp"], "tensor": mesh.shape["tensor"]}
    placed = (
        P("dp", None),
        P("dp", None),
        P("dp", None),
        P("dp", None),
        P("dp", None),
        P(None, ("dp", "tensor")),
        P(None, ("dp", "tensor")),
    )
    return jax.shard_map(
        functools.partial(shards, groups),
        mesh=mesh,
        in_specs=placed,
        out_specs=(P("dp", None), P("dp", None), P("dp", None), P(None, ("dp", "tensor")), P("dp")),
        check_vma=False,
    )
```

```python
import functools

import jax
import jax.numpy as jnp
from jax import lax
from jax.experimental import pallas as pl
from jax.experimental.pallas import tpu as pltpu
from jax.sharding import PartitionSpec as P

ROUNDS = 3
CAP = 256

TEACHER_TEMP = 0.07
STUDENT_TEMP = 0.1
EPS = 1e-06
GRAD_SCALE = 65536.0
LOG2E = 1.4426950408889634
LANES = 128
BLOCK = 512
MESH = pl.DeviceIdType.MESH
F32 = jnp.float32
BF16 = jnp.bfloat16


def gelu_parts(pre):
    cdf = 0.5 * (1.0 + lax.erf(pre * 0.7071067811865476))
    pdf = jnp.exp(-0.5 * pre * pre) * 0.3989422804014327
    return (pre * cdf, cdf + pre * pdf)


def unit_rows(feats):
    inverse = lax.rsqrt(jnp.sum(feats * feats, axis=1, keepdims=True) + EPS)
    return (feats * inverse, inverse)


def unit_columns(protos):
    wide = protos.astype(F32)
    norms = jnp.sqrt(jnp.sum(wide * wide, axis=0, keepdims=True) + EPS)
    return (wide / norms, norms)


def spread(dense, out_ref):
    for c in range(dense.shape[0]):
        row = jnp.broadcast_to(dense[c : c + 1, :], (LANES, LANES))
        out_ref[c * LANES : (c + 1) * LANES, :] = row.T


def gathered(acc_ref, out_ref, base):
    for c in range(acc_ref.shape[0] // LANES):
        turned = acc_ref[c * LANES : (c + 1) * LANES, :].T
        out_ref[base + c : base + c + 1, :] = jnp.sum(turned, axis=0, keepdims=True)


def fold_lanes(values):
    total = values[:, :LANES]
    for start in range(LANES, values.shape[1], LANES):
        total = total + values[:, start : start + LANES]
    return total


def widen(values, cols):
    return jnp.concatenate([values] * (cols // LANES), axis=1)


def chunk(step):
    return pl.ds(pl.multiple_of(step * CAP, CAP), CAP)


def two_terms(row):
    high = row.astype(BF16)
    low = (row - high.astype(F32)).astype(BF16)
    return jnp.concatenate([high, low, jnp.zeros((14, row.shape[1]), BF16)], axis=0)


def flatten(dense):
    return jnp.concatenate([dense[c : c + 1, :] for c in range(dense.shape[0])], axis=1)


def row_scale(live, row_sum):
    return live / (row_sum + 1.0 - live)


def column_scale(expo, u_terms):
    total = jnp.dot(u_terms[...], expo[...], preferred_element_type=F32)
    return 1.0 / (total[0:1, :] + total[1:2, :])


def add_row_sums(expo, scale, acc):
    terms = two_terms(scale)

    def sum_rows(step, carry):
        part = chunk(step)
        acc[part, :] += lax.dot_general(
            expo[part, :], terms, (((1,), (1,)), ((), ())), preferred_element_type=F32
        )
        return carry

    lax.fori_loop(0, expo.shape[0] // CAP, sum_rows, 0)


def first_kernel(teach, proto, live, expo, sums, u_terms, acc):
    rows, block = expo.shape
    here = pl.program_id(0)

    @pl.when(here == 0)
    def _():
        u_terms[...] = two_terms(flatten(live[...]))
        acc[...] = jnp.zeros_like(acc)

    cols = unit_columns(proto[...])[0].astype(BF16)

    def raise_rows(step, carry):
        part = chunk(step)
        cos = jnp.dot(teach[part, :], cols, preferred_element_type=F32)
        expo[part, :] = jnp.exp2(cos * (LOG2E / TEACHER_TEMP)).astype(BF16)
        return carry

    lax.fori_loop(0, rows // CAP, raise_rows, 0)
    add_row_sums(expo, column_scale(expo, u_terms), acc)

    @pl.when(here == pl.num_programs(0) - 1)
    def _():
        gathered(acc, sums, 0)


def middle_kernel(expo, live, row_sum, sums, u_terms, acc):
    here = pl.program_id(0)

    @pl.when(here == 0)
    def _():
        u_terms[...] = two_terms(flatten(row_scale(live[...], row_sum[...])))
        acc[...] = jnp.zeros_like(acc)

    add_row_sums(expo, column_scale(expo, u_terms), acc)

    @pl.when(here == pl.num_programs(0) - 1)
    def _():
        gathered(acc, sums, 0)


def last_kernel(expo, live, row_sum, student, proto, raised, v_out, sums, u_terms, acc, acc_n, acc_c):
    rows, block = expo.shape
    here = pl.program_id(0)

    @pl.when(here == 0)
    def _():
        u_terms[...] = two_terms(flatten(row_scale(live[...], row_sum[...])))
        acc[...] = jnp.zeros_like(acc)
        acc_n[...] = jnp.zeros_like(acc_n)
        acc_c[...] = jnp.zeros_like(acc_c)

    scale = column_scale(expo, u_terms)
    v_out[...] = jnp.broadcast_to(scale, v_out.shape)
    cols = unit_columns(proto[...])[0].astype(BF16)

    def sum_rows(step, carry):
        part = chunk(step)
        dots = jnp.dot(student[part, :], cols, preferred_element_type=F32)
        power = jnp.exp2(dots * (LOG2E / STUDENT_TEMP))
        raised[part, :] = power.astype(BF16)
        balanced = expo[part, :].astype(F32) * scale
        acc[part, :] += fold_lanes(balanced)
        acc_n[part, :] += fold_lanes(power)
        acc_c[part, :] += fold_lanes(balanced * dots)
        return carry

    lax.fori_loop(0, rows // CAP, sum_rows, 0)

    @pl.when(here == pl.num_programs(0) - 1)
    def _():
        dense = rows // LANES
        acc_c[...] = acc_c[...] * (1.0 / STUDENT_TEMP)
        gathered(acc, sums, 0)
        gathered(acc_n, sums, dense)
        gathered(acc_c, sums, 2 * dense)


def grad_kernel(
    expo, raised, v_in, live, weight, sums, student_t, proto, part_out, grad_out, prob_b, target_b, total, score
):
    rows, block = expo.shape
    here = pl.program_id(0)
    dense = rows // LANES

    @pl.when(here == 0)
    def _():
        factor = weight[...] * (1.0 / STUDENT_TEMP)
        spread(factor / sums[dense : 2 * dense, :], prob_b)
        spread(factor * row_scale(live[...], sums[:dense, :]), target_b)
        total[...] = jnp.zeros_like(total)

    unit, norms = unit_columns(proto[...])
    cols = unit.astype(BF16)
    scale = v_in[0:1, :]

    def one_group(step, carry):
        part = chunk(step)
        target = expo[part, :].astype(F32) * scale * widen(target_b[part, :], block)
        probs = raised[part, :].astype(F32) * widen(prob_b[part, :], block)
        value = (probs - target).astype(BF16)
        score[part, :] = value
        total[part, :] += lax.dot_general(
            value, cols, (((1,), (1,)), ((), ())), preferred_element_type=F32
        )
        return carry

    lax.fori_loop(0, rows // CAP, one_group, 0)
    grad = jnp.dot(student_t[...], score[...], preferred_element_type=F32)
    grad_out[...] = (grad - unit * jnp.sum(unit * grad, axis=0, keepdims=True)) / norms

    @pl.when(here == pl.num_programs(0) - 1)
    def _():
        part_out[...] = total[...].astype(BF16)


def whole(shape):
    return pl.BlockSpec(shape, lambda i: tuple(0 for _ in shape))


def tall(rows, block):
    return pl.BlockSpec((rows, block), lambda i: (0, i))


def params(**extra):
    return pltpu.CompilerParams(
        dimension_semantics=("arbitrary",), vmem_limit_bytes=48 * 1024 * 1024, **extra
    )


def cost(flops, moved, powers):
    return pl.CostEstimate(flops=flops, bytes_accessed=moved, transcendentals=powers)


def prototype_first(teach, proto, live):
    rows, width = teach.shape
    columns = proto.shape[1]
    block = min(BLOCK, columns)
    return pl.pallas_call(
        first_kernel,
        name="first_round",
        grid=(columns // block,),
        in_specs=[whole(teach.shape), tall(width, block), whole(live.shape)],
        out_specs=[tall(rows, block), whole(live.shape)],
        out_shape=[jax.ShapeDtypeStruct((rows, columns), BF16), jax.ShapeDtypeStruct(live.shape, F32)],
        scratch_shapes=[pltpu.VMEM((16, rows), BF16), pltpu.VMEM((rows, 16), F32)],
        compiler_params=params(),
        cost_estimate=cost(2 * rows * width * columns, 2 * rows * columns, rows * columns),
    )(teach, proto, live)


def prototype_middle(expo, live, row_sum):
    rows, columns = expo.shape
    block = min(BLOCK, columns)
    return pl.pallas_call(
        middle_kernel,
        name="middle_round",
        grid=(columns // block,),
        in_specs=[tall(rows, block), whole(live.shape), whole(live.shape)],
        out_specs=whole(live.shape),
        out_shape=jax.ShapeDtypeStruct(live.shape, F32),
        scratch_shapes=[pltpu.VMEM((16, rows), BF16), pltpu.VMEM((rows, 16), F32)],
        compiler_params=params(),
        cost_estimate=cost(4 * rows * columns, 2 * rows * columns, 0),
    )(expo, live, row_sum)


def prototype_last(expo, live, row_sum, student, proto):
    rows, columns = expo.shape
    width = student.shape[1]
    block = min(BLOCK, columns)
    dense = live.shape[0]
    return pl.pallas_call(
        last_kernel,
        name="last_round",
        grid=(columns // block,),
        in_specs=[
            tall(rows, block),
            whole(live.shape),
            whole(live.shape),
            whole(student.shape),
            tall(width, block),
        ],
        out_specs=[tall(rows, block), tall(8, block), whole((3 * dense, LANES))],
        out_shape=[
            jax.ShapeDtypeStruct((rows, columns), BF16),
            jax.ShapeDtypeStruct((8, columns), F32),
            jax.ShapeDtypeStruct((3 * dense, LANES), F32),
        ],
        scratch_shapes=[pltpu.VMEM((16, rows), BF16)] + [pltpu.VMEM((rows, LANES), F32)] * 3,
        compiler_params=params(),
        cost_estimate=cost(2 * rows * width * columns, 4 * rows * columns, rows * columns),
    )(expo, live, row_sum, student, proto)


def prototype_grad(expo, raised, v, live, weight, sums, student_t, proto):
    rows, columns = expo.shape
    width = proto.shape[0]
    block = min(BLOCK, columns)
    return pl.pallas_call(
        grad_kernel,
        name="score_grad",
        grid=(columns // block,),
        in_specs=[
            tall(rows, block),
            tall(rows, block),
            tall(8, block),
            whole(live.shape),
            whole(live.shape),
            whole(sums.shape),
            whole(student_t.shape),
            tall(width, block),
        ],
        out_specs=[whole((rows, width)), tall(width, block)],
        out_shape=[
            jax.ShapeDtypeStruct((rows, width), BF16),
            jax.ShapeDtypeStruct((width, columns), F32),
        ],
        scratch_shapes=[pltpu.VMEM((rows, LANES), F32)] * 2
        + [pltpu.VMEM((rows, width), F32), pltpu.VMEM((rows, block), BF16)],
        compiler_params=params(),
        cost_estimate=cost(4 * rows * width * columns, 4 * rows * columns, 0),
    )(expo, raised, v, live, weight, sums, student_t, proto)


def greet(groups, many):
    barrier = pltpu.get_barrier_semaphore()
    for axis in ("dp", "tensor"):
        me = lax.axis_index(axis)
        for step in range(1, groups[axis]):
            peer = lax.rem(me + step, groups[axis])
            pl.semaphore_signal(barrier, inc=1, device_id={axis: peer}, device_id_type=MESH)
    pl.semaphore_wait(barrier, many)


def copies(axis, n, source, landing, send, recv):
    me = lax.axis_index(axis)

    def copy(peer, slot):
        return pltpu.make_async_remote_copy(
            src_ref=source(peer),
            dst_ref=landing(slot),
            send_sem=send(peer),
            recv_sem=recv(slot),
            device_id={axis: peer},
            device_id_type=MESH,
        )

    def start():
        for step in range(1, n):
            copy(lax.rem(me + step, n), me).start()

    def wait():
        for step in range(1, n):
            peer = lax.rem(me + step, n)
            copy(peer, peer).wait()

    return start, wait


def exchange(axis, n, source, landing, send, recv):
    start, wait = copies(
        axis, n, source, lambda slot: landing.at[slot], lambda peer: send.at[peer], lambda slot: recv.at[slot]
    )
    start()
    wait()


def gather_kernel(groups, count, *refs):
    values, outs, (send, recv) = refs[:count], refs[count : 2 * count], refs[2 * count :]
    n = groups["dp"]
    me = lax.axis_index("dp")
    greet({"dp": n, "tensor": 1}, n - 1)
    waits = []
    for k in range(count):
        start, wait = copies(
            "dp",
            n,
            lambda peer, k=k: values[k],
            lambda slot, k=k: outs[k].at[slot],
            lambda peer, k=k: send.at[k, peer],
            lambda slot, k=k: recv.at[k, slot],
        )
        start()
        waits.append(wait)
    for k in range(count):
        outs[k][me] = values[k][...]
    for wait in waits:
        wait()


def gather_rows(values, groups, ident):
    n = groups["dp"]
    return pl.pallas_call(
        functools.partial(gather_kernel, groups, len(values)),
        name=f"gather_rows_{ident}",
        in_specs=[pl.BlockSpec(memory_space=pltpu.VMEM)] * len(values),
        out_specs=[pl.BlockSpec(memory_space=pltpu.VMEM)] * len(values),
        out_shape=[jax.ShapeDtypeStruct((n,) + value.shape, value.dtype) for value in values],
        scratch_shapes=[pltpu.SemaphoreType.DMA((len(values), n))] * 2,
        compiler_params=pltpu.CompilerParams(collective_id=ident, has_side_effects=True),
    )(*values)


def total_kernel(groups, value, out, near, far, send_a, recv_a, send_b, recv_b):
    n, m = groups["dp"], groups["tensor"]
    greet(groups, n + m - 2)
    exchange("dp", n, lambda peer: value, near, send_a, recv_a)
    near[lax.axis_index("dp")] = value[...]
    part = near[0]
    for slot in range(1, n):
        part = part + near[slot]
    out[...] = part
    exchange("tensor", m, lambda peer: out, far, send_b, recv_b)
    far[lax.axis_index("tensor")] = part
    part = far[0]
    for slot in range(1, m):
        part = part + far[slot]
    out[...] = part


def everywhere_total(value, groups, ident):
    n, m = groups["dp"], groups["tensor"]
    return pl.pallas_call(
        functools.partial(total_kernel, groups),
        name=f"row_total_{ident}",
        in_specs=[pl.BlockSpec(memory_space=pltpu.VMEM)],
        out_specs=pl.BlockSpec(memory_space=pltpu.VMEM),
        out_shape=jax.ShapeDtypeStruct(value.shape, F32),
        scratch_shapes=[
            pltpu.VMEM((n,) + value.shape, F32),
            pltpu.VMEM((m,) + value.shape, F32),
            pltpu.SemaphoreType.DMA((n,)),
            pltpu.SemaphoreType.DMA((n,)),
            pltpu.SemaphoreType.DMA((m,)),
            pltpu.SemaphoreType.DMA((m,)),
        ],
        compiler_params=pltpu.CompilerParams(collective_id=ident, has_side_effects=True),
    )(value)


def run_jobs(groups, jobs, send_a, recv_a, send_b, recv_b):
    n, m = groups["dp"], groups["tensor"]
    me = lax.axis_index("dp")
    greet(groups, n + m - 2)
    firsts, seconds = [], []
    for k, (source, near, part, far) in enumerate(jobs):
        start, wait = copies(
            "dp", n, source, near, lambda peer, k=k: send_a.at[k, peer], lambda slot, k=k: recv_a.at[k, slot]
        )
        start()
        firsts.append(wait)
    for k, (source, near, part, far) in enumerate(jobs):
        firsts[k]()
        total = source(me)[...].astype(F32)
        for step in range(1, n):
            total = total + near(lax.rem(me + step, n))[...].astype(F32)
        part[...] = total.astype(BF16)
        start, wait = copies(
            "tensor",
            m,
            lambda peer, part=part: part,
            far,
            lambda peer, k=k: send_b.at[k, peer],
            lambda slot, k=k: recv_b.at[k, slot],
        )
        start()
        far(lax.axis_index("tensor"))[...] = part[...]
        seconds.append(wait)
    for wait in seconds:
        wait()


def job_semaphores(groups, jobs):
    n, m = groups["dp"], groups["tensor"]
    return [pltpu.SemaphoreType.DMA((jobs, n))] * 2 + [pltpu.SemaphoreType.DMA((jobs, m))] * 2


OWNER_PIECES = 4


def owner_kernel(groups, value, out, near, far, part, *semaphores):
    rows = out.shape[0] // OWNER_PIECES
    jobs = []
    for k in range(OWNER_PIECES):
        piece = pl.ds(k * rows, rows)
        jobs.append(
            (
                lambda peer, piece=piece: value.at[peer, piece, :],
                lambda slot, piece=piece: near.at[slot, piece, :],
                part.at[piece, :],
                lambda slot, piece=piece: far.at[slot, piece, :],
            )
        )
    run_jobs(groups, jobs, *semaphores)
    total = far[0].astype(F32)
    for slot in range(1, groups["tensor"]):
        total = total + far[slot].astype(F32)
    out[...] = total


def owner_total(value, groups, ident):
    n, m = groups["dp"], groups["tensor"]
    own = value.shape[1:]
    return pl.pallas_call(
        functools.partial(owner_kernel, groups),
        name="owner_total",
        in_specs=[pl.BlockSpec(memory_space=pltpu.VMEM)],
        out_specs=pl.BlockSpec(memory_space=pltpu.VMEM),
        out_shape=jax.ShapeDtypeStruct(own, F32),
        scratch_shapes=[
            pltpu.VMEM((n,) + own, BF16),
            pltpu.VMEM((m,) + own, BF16),
            pltpu.VMEM(own, BF16),
        ]
        + job_semaphores(groups, OWNER_PIECES),
        compiler_params=pltpu.CompilerParams(collective_id=ident, has_side_effects=True),
    )(value)


def head_kernel(groups, wide, narrow, wide_out, narrow_out, wide_near, narrow_near, wide_part, narrow_part, *semaphores):
    mine = lax.axis_index("tensor")
    jobs = [
        (
            lambda peer: narrow.at[peer, mine],
            lambda slot: narrow_near.at[slot],
            narrow_part,
            lambda slot: narrow_out.at[slot],
        )
    ]
    for k in range(wide.shape[2] // LANES):
        piece = pl.ds(k * LANES, LANES)
        jobs.append(
            (
                lambda peer, piece=piece: wide.at[peer, :, piece],
                lambda slot, piece=piece: wide_near.at[slot, :, piece],
                wide_part.at[:, piece],
                lambda slot, piece=piece: wide_out.at[slot, :, piece],
            )
        )
    run_jobs(groups, jobs, *semaphores)


def head_totals(wide, narrow, groups, ident):
    n, m = groups["dp"], groups["tensor"]
    wide_own, narrow_own = wide.shape[1:], narrow.shape[2:]
    return pl.pallas_call(
        functools.partial(head_kernel, groups),
        name="head_totals",
        in_specs=[pl.BlockSpec(memory_space=pltpu.VMEM)] * 2,
        out_specs=[pl.BlockSpec(memory_space=pltpu.VMEM)] * 2,
        out_shape=[jax.ShapeDtypeStruct((m,) + wide_own, BF16), jax.ShapeDtypeStruct((m,) + narrow_own, BF16)],
        scratch_shapes=[
            pltpu.VMEM((n,) + wide_own, BF16),
            pltpu.VMEM((n,) + narrow_own, BF16),
            pltpu.VMEM(wide_own, BF16),
            pltpu.VMEM(narrow_own, BF16),
        ]
        + job_semaphores(groups, 1 + wide.shape[2] // LANES),
        compiler_params=pltpu.CompilerParams(collective_id=ident, has_side_effects=True),
    )(wide, narrow)


def head_forward(rows, w_in_all, w_out_all):
    pre = jnp.dot(rows, w_in_all, preferred_element_type=F32)
    act, slope = gelu_parts(pre)
    hidden = act.astype(BF16)
    feats = jnp.dot(hidden, w_out_all, preferred_element_type=F32)
    unit, inv = unit_rows(feats)
    return (hidden, slope, unit, inv, unit.astype(BF16))


def head_backward(rows, hidden, slope, unit, inv, grad_unit, w_in_all, w_out_all):
    inner = jnp.sum(unit * grad_unit, axis=1, keepdims=True)
    grad_feats = (inv * (grad_unit - unit * inner)).astype(BF16)
    grad_out_part = lax.dot_general(
        hidden, grad_feats, (((0,), (0,)), ((), ())), preferred_element_type=F32
    )
    grad_hidden = lax.dot_general(
        grad_feats, w_out_all, (((1,), (1,)), ((), ())), preferred_element_type=F32
    )
    grad_pre = (grad_hidden * slope).astype(BF16)
    width = grad_pre.shape[1] // lax.axis_size("tensor")
    own_pre = lax.dynamic_slice_in_dim(grad_pre, lax.axis_index("tensor") * width, width, axis=1)
    grad_in_part = lax.dot_general(
        rows, own_pre, (((0,), (0,)), ((), ())), preferred_element_type=F32
    )
    grad_rows = lax.dot_general(
        grad_pre, w_in_all, (((1,), (1,)), ((), ())), preferred_element_type=F32
    )
    return (grad_in_part, grad_out_part, grad_rows)


def selection(masks):
    crops, patches = masks.shape
    size = crops * patches
    flat = masks.reshape(1, size)
    before = (
        lax.broadcasted_iota(jnp.int32, (size, size), 0) < lax.broadcasted_iota(jnp.int32, (size, size), 1)
    ).astype(BF16)
    place = jnp.dot(flat.astype(BF16), before, preferred_element_type=F32).astype(jnp.int32)
    slots = lax.broadcasted_iota(jnp.int32, (CAP, size), 0)
    picked = (place == slots) & (flat > 0)
    dead = slots >= jnp.sum(flat)
    first = lax.broadcasted_iota(jnp.int32, (CAP, size), 1) == 0
    return (picked | (dead & first)).astype(BF16), picked.astype(BF16)


def shards(groups, tokens, teacher_feats, masks, w_in, w_out, proto_student, proto_teacher):
    w_in_all = lax.all_gather(w_in, "dp", axis=0, tiled=True)
    w_out_all = lax.all_gather(w_out, "dp", axis=0, tiled=True)
    pick, place = selection(masks)
    counts = jnp.sum(masks, axis=1)
    ends = jnp.sum(
        jnp.where(jnp.arange(counts.shape[0])[:, None] <= jnp.arange(counts.shape[0])[None, :], counts[:, None], 0),
        axis=0,
    )
    slot = jnp.arange(CAP)[:, None]
    member = ((slot >= (ends - counts)[None, :]) & (slot < ends[None, :])).astype(F32)
    inverse = 1.0 / jnp.maximum(counts, 1).astype(F32)
    weight = (GRAD_SCALE * jnp.sum(member * inverse[None, :], axis=1)).astype(BF16)
    teacher_pick = jnp.dot(pick, teacher_feats, preferred_element_type=F32)
    teacher_rows = unit_rows(teacher_pick)[0].astype(BF16)
    teacher_every, weight_every = gather_rows((teacher_rows, weight.astype(F32).reshape(-1, LANES)), groups, 6)
    teacher_every = teacher_every.reshape(-1, teacher_rows.shape[1])
    weight_every = weight_every.reshape(-1, LANES)
    live_every = (weight_every > 0).astype(F32)

    expo, row_sum = prototype_first(teacher_every, proto_teacher, live_every)
    row_sum = everywhere_total(row_sum, groups, 1)

    for turn in range(ROUNDS - 2):
        row_sum = prototype_middle(expo, live_every, row_sum)
        row_sum = everywhere_total(row_sum, groups, 2 + turn)

    rows = jnp.dot(pick, tokens, preferred_element_type=F32).astype(BF16)
    rows, row_sum = lax.optimization_barrier((rows, row_sum))
    hidden, slope, unit, inv, student_rows = head_forward(rows, w_in_all, w_out_all)
    (student_every,) = gather_rows((student_rows,), groups, 7)
    student_every = student_every.reshape(-1, student_rows.shape[1])

    raised, v, sums = prototype_last(expo, live_every, row_sum, student_every, proto_student)
    sums = everywhere_total(sums, groups, ROUNDS)
    grad_part, grad_proto = prototype_grad(
        expo, raised, v, live_every, weight_every, sums, student_every.T, proto_student
    )
    grad_unit = owner_total(grad_part.reshape(groups["dp"], CAP, -1), groups, ROUNDS + 1)

    dense = live_every.shape[0]
    own = CAP // LANES
    start = lax.axis_index("dp") * own

    def mine(values):
        return lax.dynamic_slice_in_dim(values, start, own).reshape(CAP)

    live_own = mine(live_every)
    scale_row = live_own / (mine(sums[:dense]) + 1.0 - live_own)
    row_loss = jnp.log(mine(sums[dense : 2 * dense])) - scale_row * mine(sums[2 * dense :])
    crop_loss = jnp.sum(member * row_loss[:, None], axis=0) * inverse

    grad_in_part, grad_out_part, grad_rows = head_backward(
        rows, hidden, slope, unit, inv, grad_unit, w_in_all, w_out_all
    )
    n, m = groups["dp"], groups["tensor"]
    wide = grad_in_part.astype(BF16).reshape(n, -1, grad_in_part.shape[1])
    narrow = grad_out_part.astype(BF16).reshape(n, m, -1, grad_out_part.shape[1])
    wide, narrow = head_totals(wide, narrow, groups, ROUNDS + 5)
    grad_in = wide.transpose(1, 0, 2).reshape(wide.shape[1], -1).astype(F32)
    grad_out = narrow.reshape(-1, narrow.shape[2]).astype(F32)
    d_tokens = lax.dot_general(
        place, grad_rows.astype(BF16), (((0,), (0,)), ((), ())), preferred_element_type=F32
    ).astype(BF16)
    return (d_tokens, grad_in, grad_out, grad_proto, crop_loss)


def solution(mesh):
    groups = {"dp": mesh.shape["dp"], "tensor": mesh.shape["tensor"]}
    placed = (
        P("dp", None),
        P("dp", None),
        P("dp", None),
        P("dp", None),
        P("dp", None),
        P(None, ("dp", "tensor")),
        P(None, ("dp", "tensor")),
    )
    return jax.shard_map(
        functools.partial(shards, groups),
        mesh=mesh,
        in_specs=placed,
        out_specs=(P("dp", None), P("dp", None), P("dp", None), P(None, ("dp", "tensor")), P("dp")),
        check_vma=False,
    )
```

```python
import functools

import jax
import jax.numpy as jnp
from jax import lax
from jax.experimental import pallas as pl
from jax.experimental.pallas import tpu as pltpu
from jax.sharding import PartitionSpec as P

ROUNDS = 3
CAP = 256

TEACHER_TEMP = 0.07
STUDENT_TEMP = 0.1
EPS = 1e-06
GRAD_SCALE = 65536.0
LOG2E = 1.4426950408889634
LANES = 128
BLOCK = 1 << 21
TILE = 256
UNROLL = 4
ROW_PRODUCT = False
MESH = pl.DeviceIdType.MESH
F32 = jnp.float32
BF16 = jnp.bfloat16


def gelu_parts(pre):
    cdf = 0.5 * (1.0 + lax.erf(pre * 0.7071067811865476))
    pdf = jnp.exp(-0.5 * pre * pre) * 0.3989422804014327
    return (pre * cdf, cdf + pre * pdf)


def unit_rows(feats):
    inverse = lax.rsqrt(jnp.sum(feats * feats, axis=1, keepdims=True) + EPS)
    return (feats * inverse, inverse)


def unit_columns(protos):
    wide = protos.astype(F32)
    norms = jnp.sqrt(jnp.sum(wide * wide, axis=0, keepdims=True) + EPS)
    return (wide / norms, norms)


def spread(dense, out_ref):
    for c in range(dense.shape[0]):
        row = jnp.broadcast_to(dense[c : c + 1, :], (LANES, LANES))
        out_ref[c * LANES : (c + 1) * LANES, :] = row.T


def gathered(acc_ref, out_ref, base):
    for c in range(acc_ref.shape[0] // LANES):
        turned = acc_ref[c * LANES : (c + 1) * LANES, :].T
        out_ref[base + c : base + c + 1, :] = jnp.sum(turned, axis=0, keepdims=True)


def fold_lanes(values):
    total = values[:, :LANES]
    for start in range(LANES, values.shape[1], LANES):
        total = total + values[:, start : start + LANES]
    return total


def widen(values, cols):
    return jnp.concatenate([values] * (cols // LANES), axis=1)


def chunk(step):
    return pl.ds(pl.multiple_of(step * TILE, TILE), TILE)


def each_tile(rows, body):
    lax.fori_loop(0, rows // TILE, body, 0, unroll=UNROLL)


def two_terms(row):
    high = row.astype(BF16)
    low = (row - high.astype(F32)).astype(BF16)
    return jnp.concatenate([high, low, jnp.zeros((14, row.shape[1]), BF16)], axis=0)


def flatten(dense):
    return jnp.concatenate([dense[c : c + 1, :] for c in range(dense.shape[0])], axis=1)


def row_scale(live, row_sum):
    return live / (row_sum + 1.0 - live)


def column_scale(expo, u_terms):
    total = jnp.dot(u_terms[...], expo[...], preferred_element_type=F32)
    return 1.0 / (total[0:1, :] + total[1:2, :])


def add_row_sums(expo, scale, acc):
    terms = two_terms(scale)

    def sum_rows(step, carry):
        part = chunk(step)
        if ROW_PRODUCT:
            acc[part, :] += lax.dot_general(
                expo[part, :], terms, (((1,), (1,)), ((), ())), preferred_element_type=F32
            )
        else:
            acc[part, :] += fold_lanes(expo[part, :].astype(F32) * scale)
        return carry

    each_tile(expo.shape[0], sum_rows)


def first_kernel(teach, proto, live, expo, sums, u_terms, acc):
    rows, block = expo.shape
    here = pl.program_id(0)

    @pl.when(here == 0)
    def _():
        u_terms[...] = two_terms(flatten(live[...]))
        acc[...] = jnp.zeros_like(acc)

    cols = unit_columns(proto[...])[0].astype(BF16)

    def raise_rows(step, carry):
        part = chunk(step)
        cos = jnp.dot(teach[part, :], cols, preferred_element_type=F32)
        expo[part, :] = jnp.exp2(cos * (LOG2E / TEACHER_TEMP)).astype(BF16)
        return carry

    each_tile(rows, raise_rows)
    add_row_sums(expo, column_scale(expo, u_terms), acc)

    @pl.when(here == pl.num_programs(0) - 1)
    def _():
        gathered(acc, sums, 0)


def middle_kernel(expo, live, row_sum, sums, u_terms, acc):
    here = pl.program_id(0)

    @pl.when(here == 0)
    def _():
        u_terms[...] = two_terms(flatten(row_scale(live[...], row_sum[...])))
        acc[...] = jnp.zeros_like(acc)

    add_row_sums(expo, column_scale(expo, u_terms), acc)

    @pl.when(here == pl.num_programs(0) - 1)
    def _():
        gathered(acc, sums, 0)


def last_kernel(expo, live, row_sum, student, proto, raised, v_out, sums, u_terms, acc, acc_n, acc_c):
    rows, block = expo.shape
    here = pl.program_id(0)

    @pl.when(here == 0)
    def _():
        u_terms[...] = two_terms(flatten(row_scale(live[...], row_sum[...])))
        acc[...] = jnp.zeros_like(acc)
        acc_n[...] = jnp.zeros_like(acc_n)
        acc_c[...] = jnp.zeros_like(acc_c)

    scale = column_scale(expo, u_terms)
    v_out[...] = jnp.broadcast_to(scale, v_out.shape)
    cols = unit_columns(proto[...])[0].astype(BF16)

    def sum_rows(step, carry):
        part = chunk(step)
        dots = jnp.dot(student[part, :], cols, preferred_element_type=F32)
        power = jnp.exp2(dots * (LOG2E / STUDENT_TEMP))
        raised[part, :] = power.astype(BF16)
        balanced = expo[part, :].astype(F32) * scale
        acc[part, :] += fold_lanes(balanced)
        acc_n[part, :] += fold_lanes(power)
        acc_c[part, :] += fold_lanes(balanced * dots)
        return carry

    each_tile(rows, sum_rows)

    @pl.when(here == pl.num_programs(0) - 1)
    def _():
        dense = rows // LANES
        acc_c[...] = acc_c[...] * (1.0 / STUDENT_TEMP)
        gathered(acc, sums, 0)
        gathered(acc_n, sums, dense)
        gathered(acc_c, sums, 2 * dense)


def grad_kernel(
    expo, raised, v_in, live, weight, sums, student_t, proto, part_out, grad_out, prob_b, target_b, total, score
):
    rows, block = expo.shape
    here = pl.program_id(0)
    dense = rows // LANES

    @pl.when(here == 0)
    def _():
        factor = weight[...] * (1.0 / STUDENT_TEMP)
        spread(factor / sums[dense : 2 * dense, :], prob_b)
        spread(factor * row_scale(live[...], sums[:dense, :]), target_b)
        total[...] = jnp.zeros_like(total)

    unit, norms = unit_columns(proto[...])
    cols = unit.astype(BF16)
    scale = v_in[0:1, :]

    def one_group(step, carry):
        part = chunk(step)
        target = expo[part, :].astype(F32) * scale * widen(target_b[part, :], block)
        probs = raised[part, :].astype(F32) * widen(prob_b[part, :], block)
        value = (probs - target).astype(BF16)
        score[part, :] = value
        total[part, :] += lax.dot_general(
            value, cols, (((1,), (1,)), ((), ())), preferred_element_type=F32
        )
        return carry

    each_tile(rows, one_group)
    grad = jnp.dot(student_t[...], score[...], preferred_element_type=F32)
    grad_out[...] = (grad - unit * jnp.sum(unit * grad, axis=0, keepdims=True)) / norms

    @pl.when(here == pl.num_programs(0) - 1)
    def _():
        part_out[...] = total[...].astype(BF16)


def whole(shape):
    return pl.BlockSpec(shape, lambda i: tuple(0 for _ in shape))


def tall(rows, block):
    return pl.BlockSpec((rows, block), lambda i: (0, i))


def params(**extra):
    return pltpu.CompilerParams(
        dimension_semantics=("arbitrary",), vmem_limit_bytes=48 * 1024 * 1024, **extra
    )


def cost(flops, moved, powers):
    return pl.CostEstimate(flops=flops, bytes_accessed=moved, transcendentals=powers)


def prototype_first(teach, proto, live):
    rows, width = teach.shape
    columns = proto.shape[1]
    block = min(BLOCK // rows, columns)
    return pl.pallas_call(
        first_kernel,
        name="first_round",
        grid=(columns // block,),
        in_specs=[whole(teach.shape), tall(width, block), whole(live.shape)],
        out_specs=[tall(rows, block), whole(live.shape)],
        out_shape=[jax.ShapeDtypeStruct((rows, columns), BF16), jax.ShapeDtypeStruct(live.shape, F32)],
        scratch_shapes=[pltpu.VMEM((16, rows), BF16), pltpu.VMEM((rows, 16 if ROW_PRODUCT else LANES), F32)],
        compiler_params=params(),
        cost_estimate=cost(2 * rows * width * columns, 2 * rows * columns, rows * columns),
    )(teach, proto, live)


def prototype_middle(expo, live, row_sum):
    rows, columns = expo.shape
    block = min(BLOCK // rows, columns)
    return pl.pallas_call(
        middle_kernel,
        name="middle_round",
        grid=(columns // block,),
        in_specs=[tall(rows, block), whole(live.shape), whole(live.shape)],
        out_specs=whole(live.shape),
        out_shape=jax.ShapeDtypeStruct(live.shape, F32),
        scratch_shapes=[pltpu.VMEM((16, rows), BF16), pltpu.VMEM((rows, 16 if ROW_PRODUCT else LANES), F32)],
        compiler_params=params(),
        cost_estimate=cost(4 * rows * columns, 2 * rows * columns, 0),
    )(expo, live, row_sum)


def prototype_last(expo, live, row_sum, student, proto):
    rows, columns = expo.shape
    width = student.shape[1]
    block = min(BLOCK // rows, columns)
    dense = live.shape[0]
    return pl.pallas_call(
        last_kernel,
        name="last_round",
        grid=(columns // block,),
        in_specs=[
            tall(rows, block),
            whole(live.shape),
            whole(live.shape),
            whole(student.shape),
            tall(width, block),
        ],
        out_specs=[tall(rows, block), tall(8, block), whole((3 * dense, LANES))],
        out_shape=[
            jax.ShapeDtypeStruct((rows, columns), BF16),
            jax.ShapeDtypeStruct((8, columns), F32),
            jax.ShapeDtypeStruct((3 * dense, LANES), F32),
        ],
        scratch_shapes=[pltpu.VMEM((16, rows), BF16)] + [pltpu.VMEM((rows, LANES), F32)] * 3,
        compiler_params=params(),
        cost_estimate=cost(2 * rows * width * columns, 4 * rows * columns, rows * columns),
    )(expo, live, row_sum, student, proto)


def prototype_grad(expo, raised, v, live, weight, sums, student_t, proto):
    rows, columns = expo.shape
    width = proto.shape[0]
    block = min(BLOCK // rows, columns)
    return pl.pallas_call(
        grad_kernel,
        name="score_grad",
        grid=(columns // block,),
        in_specs=[
            tall(rows, block),
            tall(rows, block),
            tall(8, block),
            whole(live.shape),
            whole(live.shape),
            whole(sums.shape),
            whole(student_t.shape),
            tall(width, block),
        ],
        out_specs=[whole((rows, width)), tall(width, block)],
        out_shape=[
            jax.ShapeDtypeStruct((rows, width), BF16),
            jax.ShapeDtypeStruct((width, columns), F32),
        ],
        scratch_shapes=[pltpu.VMEM((rows, LANES), F32)] * 2
        + [pltpu.VMEM((rows, width), F32), pltpu.VMEM((rows, block), BF16)],
        compiler_params=params(),
        cost_estimate=cost(4 * rows * width * columns, 4 * rows * columns, 0),
    )(expo, raised, v, live, weight, sums, student_t, proto)


def greet(groups, many):
    barrier = pltpu.get_barrier_semaphore()
    for axis in ("dp", "tensor"):
        me = lax.axis_index(axis)
        for step in range(1, groups[axis]):
            peer = lax.rem(me + step, groups[axis])
            pl.semaphore_signal(barrier, inc=1, device_id={axis: peer}, device_id_type=MESH)
    pl.semaphore_wait(barrier, many)


def copies(axis, n, source, landing, send, recv):
    me = lax.axis_index(axis)

    def copy(peer, slot):
        return pltpu.make_async_remote_copy(
            src_ref=source(peer),
            dst_ref=landing(slot),
            send_sem=send(peer),
            recv_sem=recv(slot),
            device_id={axis: peer},
            device_id_type=MESH,
        )

    def start():
        for step in range(1, n):
            copy(lax.rem(me + step, n), me).start()

    def wait():
        for step in range(1, n):
            peer = lax.rem(me + step, n)
            copy(peer, peer).wait()

    return start, wait


def exchange(axis, n, source, landing, send, recv):
    start, wait = copies(
        axis, n, source, lambda slot: landing.at[slot], lambda peer: send.at[peer], lambda slot: recv.at[slot]
    )
    start()
    wait()


def gather_kernel(groups, count, *refs):
    values, outs, (send, recv) = refs[:count], refs[count : 2 * count], refs[2 * count :]
    n = groups["dp"]
    me = lax.axis_index("dp")
    greet({"dp": n, "tensor": 1}, n - 1)
    waits = []
    for k in range(count):
        start, wait = copies(
            "dp",
            n,
            lambda peer, k=k: values[k],
            lambda slot, k=k: outs[k].at[slot],
            lambda peer, k=k: send.at[k, peer],
            lambda slot, k=k: recv.at[k, slot],
        )
        start()
        waits.append(wait)
    for k in range(count):
        outs[k][me] = values[k][...]
    for wait in waits:
        wait()


def gather_rows(values, groups, ident):
    n = groups["dp"]
    return pl.pallas_call(
        functools.partial(gather_kernel, groups, len(values)),
        name=f"gather_rows_{ident}",
        in_specs=[pl.BlockSpec(memory_space=pltpu.VMEM)] * len(values),
        out_specs=[pl.BlockSpec(memory_space=pltpu.VMEM)] * len(values),
        out_shape=[jax.ShapeDtypeStruct((n,) + value.shape, value.dtype) for value in values],
        scratch_shapes=[pltpu.SemaphoreType.DMA((len(values), n))] * 2,
        compiler_params=pltpu.CompilerParams(collective_id=ident, has_side_effects=True),
    )(*values)


def total_kernel(groups, value, out, near, far, send_a, recv_a, send_b, recv_b):
    n, m = groups["dp"], groups["tensor"]
    greet(groups, n + m - 2)
    exchange("dp", n, lambda peer: value, near, send_a, recv_a)
    near[lax.axis_index("dp")] = value[...]
    part = near[0]
    for slot in range(1, n):
        part = part + near[slot]
    out[...] = part
    exchange("tensor", m, lambda peer: out, far, send_b, recv_b)
    far[lax.axis_index("tensor")] = part
    part = far[0]
    for slot in range(1, m):
        part = part + far[slot]
    out[...] = part


def everywhere_total(value, groups, ident):
    n, m = groups["dp"], groups["tensor"]
    return pl.pallas_call(
        functools.partial(total_kernel, groups),
        name=f"row_total_{ident}",
        in_specs=[pl.BlockSpec(memory_space=pltpu.VMEM)],
        out_specs=pl.BlockSpec(memory_space=pltpu.VMEM),
        out_shape=jax.ShapeDtypeStruct(value.shape, F32),
        scratch_shapes=[
            pltpu.VMEM((n,) + value.shape, F32),
            pltpu.VMEM((m,) + value.shape, F32),
            pltpu.SemaphoreType.DMA((n,)),
            pltpu.SemaphoreType.DMA((n,)),
            pltpu.SemaphoreType.DMA((m,)),
            pltpu.SemaphoreType.DMA((m,)),
        ],
        compiler_params=pltpu.CompilerParams(collective_id=ident, has_side_effects=True),
    )(value)


def run_jobs(groups, jobs, send_a, recv_a, send_b, recv_b):
    n, m = groups["dp"], groups["tensor"]
    me = lax.axis_index("dp")
    greet(groups, n + m - 2)
    firsts, seconds = [], []
    for k, (source, near, part, far) in enumerate(jobs):
        start, wait = copies(
            "dp", n, source, near, lambda peer, k=k: send_a.at[k, peer], lambda slot, k=k: recv_a.at[k, slot]
        )
        start()
        firsts.append(wait)
    for k, (source, near, part, far) in enumerate(jobs):
        firsts[k]()
        total = source(me)[...].astype(F32)
        for step in range(1, n):
            total = total + near(lax.rem(me + step, n))[...].astype(F32)
        part[...] = total.astype(BF16)
        start, wait = copies(
            "tensor",
            m,
            lambda peer, part=part: part,
            far,
            lambda peer, k=k: send_b.at[k, peer],
            lambda slot, k=k: recv_b.at[k, slot],
        )
        start()
        far(lax.axis_index("tensor"))[...] = part[...]
        seconds.append(wait)
    for wait in seconds:
        wait()


def job_semaphores(groups, jobs):
    n, m = groups["dp"], groups["tensor"]
    return [pltpu.SemaphoreType.DMA((jobs, n))] * 2 + [pltpu.SemaphoreType.DMA((jobs, m))] * 2


OWNER_PIECES = 4


def owner_kernel(groups, value, out, near, far, part, *semaphores):
    rows = out.shape[0] // OWNER_PIECES
    jobs = []
    for k in range(OWNER_PIECES):
        piece = pl.ds(k * rows, rows)
        jobs.append(
            (
                lambda peer, piece=piece: value.at[peer, piece, :],
                lambda slot, piece=piece: near.at[slot, piece, :],
                part.at[piece, :],
                lambda slot, piece=piece: far.at[slot, piece, :],
            )
        )
    run_jobs(groups, jobs, *semaphores)
    total = far[0].astype(F32)
    for slot in range(1, groups["tensor"]):
        total = total + far[slot].astype(F32)
    out[...] = total


def owner_total(value, groups, ident):
    n, m = groups["dp"], groups["tensor"]
    own = value.shape[1:]
    return pl.pallas_call(
        functools.partial(owner_kernel, groups),
        name="owner_total",
        in_specs=[pl.BlockSpec(memory_space=pltpu.VMEM)],
        out_specs=pl.BlockSpec(memory_space=pltpu.VMEM),
        out_shape=jax.ShapeDtypeStruct(own, F32),
        scratch_shapes=[
            pltpu.VMEM((n,) + own, BF16),
            pltpu.VMEM((m,) + own, BF16),
            pltpu.VMEM(own, BF16),
        ]
        + job_semaphores(groups, OWNER_PIECES),
        compiler_params=pltpu.CompilerParams(collective_id=ident, has_side_effects=True),
    )(value)


def head_kernel(groups, wide, narrow, wide_out, narrow_out, wide_near, narrow_near, wide_part, narrow_part, *semaphores):
    mine = lax.axis_index("tensor")
    jobs = [
        (
            lambda peer: narrow.at[peer, mine],
            lambda slot: narrow_near.at[slot],
            narrow_part,
            lambda slot: narrow_out.at[slot],
        )
    ]
    for k in range(wide.shape[2] // LANES):
        piece = pl.ds(k * LANES, LANES)
        jobs.append(
            (
                lambda peer, piece=piece: wide.at[peer, :, piece],
                lambda slot, piece=piece: wide_near.at[slot, :, piece],
                wide_part.at[:, piece],
                lambda slot, piece=piece: wide_out.at[slot, :, piece],
            )
        )
    run_jobs(groups, jobs, *semaphores)


def head_totals(wide, narrow, groups, ident):
    n, m = groups["dp"], groups["tensor"]
    wide_own, narrow_own = wide.shape[1:], narrow.shape[2:]
    return pl.pallas_call(
        functools.partial(head_kernel, groups),
        name="head_totals",
        in_specs=[pl.BlockSpec(memory_space=pltpu.VMEM)] * 2,
        out_specs=[pl.BlockSpec(memory_space=pltpu.VMEM)] * 2,
        out_shape=[jax.ShapeDtypeStruct((m,) + wide_own, BF16), jax.ShapeDtypeStruct((m,) + narrow_own, BF16)],
        scratch_shapes=[
            pltpu.VMEM((n,) + wide_own, BF16),
            pltpu.VMEM((n,) + narrow_own, BF16),
            pltpu.VMEM(wide_own, BF16),
            pltpu.VMEM(narrow_own, BF16),
        ]
        + job_semaphores(groups, 1 + wide.shape[2] // LANES),
        compiler_params=pltpu.CompilerParams(collective_id=ident, has_side_effects=True),
    )(wide, narrow)


def head_forward(rows, w_in_all, w_out_all):
    pre = jnp.dot(rows, w_in_all, preferred_element_type=F32)
    act, slope = gelu_parts(pre)
    hidden = act.astype(BF16)
    feats = jnp.dot(hidden, w_out_all, preferred_element_type=F32)
    unit, inv = unit_rows(feats)
    return (hidden, slope, unit, inv, unit.astype(BF16))


def head_backward(rows, hidden, slope, unit, inv, grad_unit, w_in_all, w_out_all):
    inner = jnp.sum(unit * grad_unit, axis=1, keepdims=True)
    grad_feats = (inv * (grad_unit - unit * inner)).astype(BF16)
    grad_out_part = lax.dot_general(
        hidden, grad_feats, (((0,), (0,)), ((), ())), preferred_element_type=F32
    )
    grad_hidden = lax.dot_general(
        grad_feats, w_out_all, (((1,), (1,)), ((), ())), preferred_element_type=F32
    )
    grad_pre = (grad_hidden * slope).astype(BF16)
    width = grad_pre.shape[1] // lax.axis_size("tensor")
    own_pre = lax.dynamic_slice_in_dim(grad_pre, lax.axis_index("tensor") * width, width, axis=1)
    grad_in_part = lax.dot_general(
        rows, own_pre, (((0,), (0,)), ((), ())), preferred_element_type=F32
    )
    grad_rows = lax.dot_general(
        grad_pre, w_in_all, (((1,), (1,)), ((), ())), preferred_element_type=F32
    )
    return (grad_in_part, grad_out_part, grad_rows)


def selection(masks):
    crops, patches = masks.shape
    size = crops * patches
    flat = masks.reshape(1, size)
    before = (
        lax.broadcasted_iota(jnp.int32, (size, size), 0) < lax.broadcasted_iota(jnp.int32, (size, size), 1)
    ).astype(BF16)
    place = jnp.dot(flat.astype(BF16), before, preferred_element_type=F32).astype(jnp.int32)
    slots = lax.broadcasted_iota(jnp.int32, (CAP, size), 0)
    picked = (place == slots) & (flat > 0)
    dead = slots >= jnp.sum(flat)
    first = lax.broadcasted_iota(jnp.int32, (CAP, size), 1) == 0
    return (picked | (dead & first)).astype(BF16), picked.astype(BF16)


def shards(groups, tokens, teacher_feats, masks, w_in, w_out, proto_student, proto_teacher):
    pick, place = selection(masks)
    counts = jnp.sum(masks, axis=1)
    ends = jnp.sum(
        jnp.where(jnp.arange(counts.shape[0])[:, None] <= jnp.arange(counts.shape[0])[None, :], counts[:, None], 0),
        axis=0,
    )
    slot = jnp.arange(CAP)[:, None]
    member = ((slot >= (ends - counts)[None, :]) & (slot < ends[None, :])).astype(F32)
    inverse = 1.0 / jnp.maximum(counts, 1).astype(F32)
    weight = (GRAD_SCALE * jnp.sum(member * inverse[None, :], axis=1)).astype(BF16)
    teacher_pick = jnp.dot(pick, teacher_feats, preferred_element_type=F32)
    teacher_rows = unit_rows(teacher_pick)[0].astype(BF16)
    teacher_every, weight_every = gather_rows((teacher_rows, weight.astype(F32).reshape(-1, LANES)), groups, 6)
    teacher_every, w_in, w_out = lax.optimization_barrier((teacher_every, w_in, w_out))
    w_in_all = lax.all_gather(w_in, "dp", axis=0, tiled=True)
    w_out_all = lax.all_gather(w_out, "dp", axis=0, tiled=True)
    teacher_every = teacher_every.reshape(-1, teacher_rows.shape[1])
    weight_every = weight_every.reshape(-1, LANES)
    live_every = (weight_every > 0).astype(F32)

    expo, row_sum = prototype_first(teacher_every, proto_teacher, live_every)
    row_sum = everywhere_total(row_sum, groups, 1)

    for turn in range(ROUNDS - 2):
        row_sum = prototype_middle(expo, live_every, row_sum)
        row_sum = everywhere_total(row_sum, groups, 2 + turn)

    rows = jnp.dot(pick, tokens, preferred_element_type=F32).astype(BF16)
    rows, row_sum = lax.optimization_barrier((rows, row_sum))
    hidden, slope, unit, inv, student_rows = head_forward(rows, w_in_all, w_out_all)
    (student_every,) = gather_rows((student_rows,), groups, 7)
    student_every = student_every.reshape(-1, student_rows.shape[1])

    raised, v, sums = prototype_last(expo, live_every, row_sum, student_every, proto_student)
    sums = everywhere_total(sums, groups, ROUNDS)
    grad_part, grad_proto = prototype_grad(
        expo, raised, v, live_every, weight_every, sums, student_every.T, proto_student
    )
    grad_unit = owner_total(grad_part.reshape(groups["dp"], CAP, -1), groups, ROUNDS + 1)

    dense = live_every.shape[0]
    own = CAP // LANES
    start = lax.axis_index("dp") * own

    def mine(values):
        return lax.dynamic_slice_in_dim(values, start, own).reshape(CAP)

    live_own = mine(live_every)
    scale_row = live_own / (mine(sums[:dense]) + 1.0 - live_own)
    row_loss = jnp.log(mine(sums[dense : 2 * dense])) - scale_row * mine(sums[2 * dense :])
    crop_loss = jnp.sum(member * row_loss[:, None], axis=0) * inverse

    grad_in_part, grad_out_part, grad_rows = head_backward(
        rows, hidden, slope, unit, inv, grad_unit, w_in_all, w_out_all
    )
    n, m = groups["dp"], groups["tensor"]
    wide = grad_in_part.astype(BF16).reshape(n, -1, grad_in_part.shape[1])
    narrow = grad_out_part.astype(BF16).reshape(n, m, -1, grad_out_part.shape[1])
    wide, narrow = head_totals(wide, narrow, groups, ROUNDS + 5)
    grad_in = wide.transpose(1, 0, 2).reshape(wide.shape[1], -1).astype(F32)
    grad_out = narrow.reshape(-1, narrow.shape[2]).astype(F32)
    d_tokens = lax.dot_general(
        place, grad_rows.astype(BF16), (((0,), (0,)), ((), ())), preferred_element_type=F32
    ).astype(BF16)
    return (d_tokens, grad_in, grad_out, grad_proto, crop_loss)


def solution(mesh):
    groups = {"dp": mesh.shape["dp"], "tensor": mesh.shape["tensor"]}
    placed = (
        P("dp", None),
        P("dp", None),
        P("dp", None),
        P("dp", None),
        P("dp", None),
        P(None, ("dp", "tensor")),
        P(None, ("dp", "tensor")),
    )
    return jax.shard_map(
        functools.partial(shards, groups),
        mesh=mesh,
        in_specs=placed,
        out_specs=(P("dp", None), P("dp", None), P("dp", None), P(None, ("dp", "tensor")), P("dp")),
        check_vma=False,
    )
```

```python
import functools

import jax
import jax.numpy as jnp
from jax import lax
from jax.experimental import pallas as pl
from jax.experimental.pallas import tpu as pltpu
from jax.sharding import PartitionSpec as P

ROUNDS = 3
CAP = 256

TEACHER_TEMP = 0.07
STUDENT_TEMP = 0.1
EPS = 1e-06
GRAD_SCALE = 65536.0
LOG2E = 1.4426950408889634
LANES = 128
BLOCK = 1 << 21
TILE = 256
UNROLL = 4
ROW_PRODUCT = False
MESH = pl.DeviceIdType.MESH
F32 = jnp.float32
BF16 = jnp.bfloat16


def gelu_parts(pre):
    cdf = 0.5 * (1.0 + lax.erf(pre * 0.7071067811865476))
    pdf = jnp.exp(-0.5 * pre * pre) * 0.3989422804014327
    return (pre * cdf, cdf + pre * pdf)


def unit_rows(feats):
    inverse = lax.rsqrt(jnp.sum(feats * feats, axis=1, keepdims=True) + EPS)
    return (feats * inverse, inverse)


def unit_columns(protos):
    wide = protos.astype(F32)
    norms = jnp.sqrt(jnp.sum(wide * wide, axis=0, keepdims=True) + EPS)
    return (wide / norms, norms)


def spread(dense, out_ref):
    for c in range(dense.shape[0]):
        row = jnp.broadcast_to(dense[c : c + 1, :], (LANES, LANES))
        out_ref[c * LANES : (c + 1) * LANES, :] = row.T


def gathered(acc_ref, out_ref, base):
    for c in range(acc_ref.shape[0] // LANES):
        turned = acc_ref[c * LANES : (c + 1) * LANES, :].T
        out_ref[base + c : base + c + 1, :] = jnp.sum(turned, axis=0, keepdims=True)


def fold_lanes(values):
    total = values[:, :LANES]
    for start in range(LANES, values.shape[1], LANES):
        total = total + values[:, start : start + LANES]
    return total


def widen(values, cols):
    return jnp.concatenate([values] * (cols // LANES), axis=1)


def chunk(step):
    return pl.ds(pl.multiple_of(step * TILE, TILE), TILE)


def each_tile(rows, body):
    lax.fori_loop(0, rows // TILE, body, 0, unroll=UNROLL)


def two_terms(row):
    high = row.astype(BF16)
    low = (row - high.astype(F32)).astype(BF16)
    return jnp.concatenate([high, low, jnp.zeros((14, row.shape[1]), BF16)], axis=0)


def flatten(dense):
    return jnp.concatenate([dense[c : c + 1, :] for c in range(dense.shape[0])], axis=1)


def row_scale(live, row_sum):
    return live / (row_sum + 1.0 - live)


def column_scale(expo, u_terms):
    total = jnp.dot(u_terms[...], expo[...], preferred_element_type=F32)
    return 1.0 / (total[0:1, :] + total[1:2, :])


def add_row_sums(expo, scale, acc):
    terms = two_terms(scale)

    def sum_rows(step, carry):
        part = chunk(step)
        if ROW_PRODUCT:
            acc[part, :] += lax.dot_general(
                expo[part, :], terms, (((1,), (1,)), ((), ())), preferred_element_type=F32
            )
        else:
            acc[part, :] += fold_lanes(expo[part, :].astype(F32) * scale)
        return carry

    each_tile(expo.shape[0], sum_rows)


def first_kernel(teach, proto, live, expo, sums, u_terms, acc):
    rows, block = expo.shape
    here = pl.program_id(0)

    @pl.when(here == 0)
    def _():
        u_terms[...] = two_terms(flatten(live[...]))
        acc[...] = jnp.zeros_like(acc)

    cols = unit_columns(proto[...])[0].astype(BF16)

    def raise_rows(step, carry):
        part = chunk(step)
        cos = jnp.dot(teach[part, :], cols, preferred_element_type=F32)
        expo[part, :] = jnp.exp2(cos * (LOG2E / TEACHER_TEMP)).astype(BF16)
        return carry

    each_tile(rows, raise_rows)
    add_row_sums(expo, column_scale(expo, u_terms), acc)

    @pl.when(here == pl.num_programs(0) - 1)
    def _():
        gathered(acc, sums, 0)


def middle_kernel(expo, live, row_sum, sums, u_terms, acc):
    here = pl.program_id(0)

    @pl.when(here == 0)
    def _():
        u_terms[...] = two_terms(flatten(row_scale(live[...], row_sum[...])))
        acc[...] = jnp.zeros_like(acc)

    add_row_sums(expo, column_scale(expo, u_terms), acc)

    @pl.when(here == pl.num_programs(0) - 1)
    def _():
        gathered(acc, sums, 0)


def last_kernel(expo, live, row_sum, student, proto, raised, v_out, sums, u_terms, acc, acc_n, acc_c):
    rows, block = expo.shape
    here = pl.program_id(0)

    @pl.when(here == 0)
    def _():
        u_terms[...] = two_terms(flatten(row_scale(live[...], row_sum[...])))
        acc[...] = jnp.zeros_like(acc)
        acc_n[...] = jnp.zeros_like(acc_n)
        acc_c[...] = jnp.zeros_like(acc_c)

    scale = column_scale(expo, u_terms)
    v_out[...] = jnp.broadcast_to(scale, v_out.shape)
    cols = unit_columns(proto[...])[0].astype(BF16)

    def sum_rows(step, carry):
        part = chunk(step)
        dots = jnp.dot(student[part, :], cols, preferred_element_type=F32)
        power = jnp.exp2(dots * (LOG2E / STUDENT_TEMP))
        raised[part, :] = power.astype(BF16)
        balanced = expo[part, :].astype(F32) * scale
        acc[part, :] += fold_lanes(balanced)
        acc_n[part, :] += fold_lanes(power)
        acc_c[part, :] += fold_lanes(balanced * dots)
        return carry

    each_tile(rows, sum_rows)

    @pl.when(here == pl.num_programs(0) - 1)
    def _():
        dense = rows // LANES
        acc_c[...] = acc_c[...] * (1.0 / STUDENT_TEMP)
        gathered(acc, sums, 0)
        gathered(acc_n, sums, dense)
        gathered(acc_c, sums, 2 * dense)


def grad_kernel(
    expo, raised, v_in, live, weight, sums, student_t, proto, part_out, grad_out, prob_b, target_b, total, score
):
    rows, block = expo.shape
    here = pl.program_id(0)
    dense = rows // LANES

    @pl.when(here == 0)
    def _():
        factor = weight[...] * (1.0 / STUDENT_TEMP)
        spread(factor / sums[dense : 2 * dense, :], prob_b)
        spread(factor * row_scale(live[...], sums[:dense, :]), target_b)
        total[...] = jnp.zeros_like(total)

    unit, norms = unit_columns(proto[...])
    cols = unit.astype(BF16)
    scale = v_in[0:1, :]

    def one_group(step, carry):
        part = chunk(step)
        target = expo[part, :].astype(F32) * scale * widen(target_b[part, :], block)
        probs = raised[part, :].astype(F32) * widen(prob_b[part, :], block)
        value = (probs - target).astype(BF16)
        score[part, :] = value
        total[part, :] += lax.dot_general(
            value, cols, (((1,), (1,)), ((), ())), preferred_element_type=F32
        )
        return carry

    each_tile(rows, one_group)
    grad = jnp.dot(student_t[...], score[...], preferred_element_type=F32)
    grad_out[...] = (grad - unit * jnp.sum(unit * grad, axis=0, keepdims=True)) / norms

    @pl.when(here == pl.num_programs(0) - 1)
    def _():
        part_out[...] = total[...].astype(BF16)


def whole(shape):
    return pl.BlockSpec(shape, lambda i: tuple(0 for _ in shape))


def tall(rows, block):
    return pl.BlockSpec((rows, block), lambda i: (0, i))


def params(**extra):
    return pltpu.CompilerParams(
        dimension_semantics=("arbitrary",), vmem_limit_bytes=48 * 1024 * 1024, **extra
    )


def cost(flops, moved, powers):
    return pl.CostEstimate(flops=flops, bytes_accessed=moved, transcendentals=powers)


def prototype_first(teach, proto, live):
    rows, width = teach.shape
    columns = proto.shape[1]
    block = min(BLOCK // rows, columns)
    return pl.pallas_call(
        first_kernel,
        name="first_round",
        grid=(columns // block,),
        in_specs=[whole(teach.shape), tall(width, block), whole(live.shape)],
        out_specs=[tall(rows, block), whole(live.shape)],
        out_shape=[jax.ShapeDtypeStruct((rows, columns), BF16), jax.ShapeDtypeStruct(live.shape, F32)],
        scratch_shapes=[pltpu.VMEM((16, rows), BF16), pltpu.VMEM((rows, 16 if ROW_PRODUCT else LANES), F32)],
        compiler_params=params(),
        cost_estimate=cost(2 * rows * width * columns, 2 * rows * columns, rows * columns),
    )(teach, proto, live)


def prototype_middle(expo, live, row_sum):
    rows, columns = expo.shape
    block = min(BLOCK // rows, columns)
    return pl.pallas_call(
        middle_kernel,
        name="middle_round",
        grid=(columns // block,),
        in_specs=[tall(rows, block), whole(live.shape), whole(live.shape)],
        out_specs=whole(live.shape),
        out_shape=jax.ShapeDtypeStruct(live.shape, F32),
        scratch_shapes=[pltpu.VMEM((16, rows), BF16), pltpu.VMEM((rows, 16 if ROW_PRODUCT else LANES), F32)],
        compiler_params=params(),
        cost_estimate=cost(4 * rows * columns, 2 * rows * columns, 0),
    )(expo, live, row_sum)


def prototype_last(expo, live, row_sum, student, proto):
    rows, columns = expo.shape
    width = student.shape[1]
    block = min(BLOCK // rows, columns)
    dense = live.shape[0]
    return pl.pallas_call(
        last_kernel,
        name="last_round",
        grid=(columns // block,),
        in_specs=[
            tall(rows, block),
            whole(live.shape),
            whole(live.shape),
            whole(student.shape),
            tall(width, block),
        ],
        out_specs=[tall(rows, block), tall(8, block), whole((3 * dense, LANES))],
        out_shape=[
            jax.ShapeDtypeStruct((rows, columns), BF16),
            jax.ShapeDtypeStruct((8, columns), F32),
            jax.ShapeDtypeStruct((3 * dense, LANES), F32),
        ],
        scratch_shapes=[pltpu.VMEM((16, rows), BF16)] + [pltpu.VMEM((rows, LANES), F32)] * 3,
        compiler_params=params(),
        cost_estimate=cost(2 * rows * width * columns, 4 * rows * columns, rows * columns),
    )(expo, live, row_sum, student, proto)


def prototype_grad(expo, raised, v, live, weight, sums, student_t, proto):
    rows, columns = expo.shape
    width = proto.shape[0]
    block = min(BLOCK // rows, columns)
    return pl.pallas_call(
        grad_kernel,
        name="score_grad",
        grid=(columns // block,),
        in_specs=[
            tall(rows, block),
            tall(rows, block),
            tall(8, block),
            whole(live.shape),
            whole(live.shape),
            whole(sums.shape),
            whole(student_t.shape),
            tall(width, block),
        ],
        out_specs=[whole((rows, width)), tall(width, block)],
        out_shape=[
            jax.ShapeDtypeStruct((rows, width), BF16),
            jax.ShapeDtypeStruct((width, columns), F32),
        ],
        scratch_shapes=[pltpu.VMEM((rows, LANES), F32)] * 2
        + [pltpu.VMEM((rows, width), F32), pltpu.VMEM((rows, block), BF16)],
        compiler_params=params(),
        cost_estimate=cost(4 * rows * width * columns, 4 * rows * columns, 0),
    )(expo, raised, v, live, weight, sums, student_t, proto)


def greet(groups, many):
    barrier = pltpu.get_barrier_semaphore()
    for axis in ("dp", "tensor"):
        me = lax.axis_index(axis)
        for step in range(1, groups[axis]):
            peer = lax.rem(me + step, groups[axis])
            pl.semaphore_signal(barrier, inc=1, device_id={axis: peer}, device_id_type=MESH)
    pl.semaphore_wait(barrier, many)


def copies(axis, n, source, landing, send, recv):
    me = lax.axis_index(axis)

    def copy(peer, slot):
        return pltpu.make_async_remote_copy(
            src_ref=source(peer),
            dst_ref=landing(slot),
            send_sem=send(peer),
            recv_sem=recv(slot),
            device_id={axis: peer},
            device_id_type=MESH,
        )

    def start():
        for step in range(1, n):
            copy(lax.rem(me + step, n), me).start()

    def wait():
        for step in range(1, n):
            peer = lax.rem(me + step, n)
            copy(peer, peer).wait()

    return start, wait


def exchange(axis, n, source, landing, send, recv):
    start, wait = copies(
        axis, n, source, lambda slot: landing.at[slot], lambda peer: send.at[peer], lambda slot: recv.at[slot]
    )
    start()
    wait()


def gather_kernel(groups, count, *refs):
    values, outs, (send, recv) = refs[:count], refs[count : 2 * count], refs[2 * count :]
    n = groups["dp"]
    me = lax.axis_index("dp")
    greet({"dp": n, "tensor": 1}, n - 1)
    flip = 1 - 2 * lax.rem(me, 2)
    partner = me + flip
    peers = [lax.rem(me + step, n) for step in range(2, n, 2)]

    def copy(k, source, slot, sender, peer):
        return pltpu.make_async_remote_copy(
            src_ref=source,
            dst_ref=outs[k].at[slot],
            send_sem=send.at[k, sender],
            recv_sem=recv.at[k, slot],
            device_id={"dp": peer},
            device_id_type=MESH,
        )

    for k in range(count):
        for peer in peers + [partner]:
            copy(k, values[k], me, peer, peer).start()
        outs[k][me] = values[k][...]
    for peer in peers:
        for k in range(count):
            copy(k, values[k], peer, peer, peer).wait_recv()
            copy(k, outs[k].at[peer], peer, peer + flip, partner).start()
    for k in range(count):
        copy(k, values[k], partner, partner, partner).wait()
        for peer in peers:
            copy(k, values[k], me, peer, peer).wait_send()
            copy(k, outs[k].at[peer], peer + flip, peer + flip, partner).wait()


def gather_rows(values, groups, ident):
    n = groups["dp"]
    return pl.pallas_call(
        functools.partial(gather_kernel, groups, len(values)),
        name=f"gather_rows_{ident}",
        in_specs=[pl.BlockSpec(memory_space=pltpu.VMEM)] * len(values),
        out_specs=[pl.BlockSpec(memory_space=pltpu.VMEM)] * len(values),
        out_shape=[jax.ShapeDtypeStruct((n,) + value.shape, value.dtype) for value in values],
        scratch_shapes=[pltpu.SemaphoreType.DMA((len(values), n))] * 2,
        compiler_params=pltpu.CompilerParams(collective_id=ident, has_side_effects=True),
    )(*values)


def total_kernel(groups, value, out, near, far, send_a, recv_a, send_b, recv_b):
    n, m = groups["dp"], groups["tensor"]
    greet(groups, n + m - 2)
    exchange("dp", n, lambda peer: value, near, send_a, recv_a)
    near[lax.axis_index("dp")] = value[...]
    part = near[0]
    for slot in range(1, n):
        part = part + near[slot]
    out[...] = part
    exchange("tensor", m, lambda peer: out, far, send_b, recv_b)
    far[lax.axis_index("tensor")] = part
    part = far[0]
    for slot in range(1, m):
        part = part + far[slot]
    out[...] = part


def everywhere_total(value, groups, ident):
    n, m = groups["dp"], groups["tensor"]
    return pl.pallas_call(
        functools.partial(total_kernel, groups),
        name=f"row_total_{ident}",
        in_specs=[pl.BlockSpec(memory_space=pltpu.VMEM)],
        out_specs=pl.BlockSpec(memory_space=pltpu.VMEM),
        out_shape=jax.ShapeDtypeStruct(value.shape, F32),
        scratch_shapes=[
            pltpu.VMEM((n,) + value.shape, F32),
            pltpu.VMEM((m,) + value.shape, F32),
            pltpu.SemaphoreType.DMA((n,)),
            pltpu.SemaphoreType.DMA((n,)),
            pltpu.SemaphoreType.DMA((m,)),
            pltpu.SemaphoreType.DMA((m,)),
        ],
        compiler_params=pltpu.CompilerParams(collective_id=ident, has_side_effects=True),
    )(value)


def run_jobs(groups, jobs, send_a, recv_a, send_b, recv_b):
    n, m = groups["dp"], groups["tensor"]
    me = lax.axis_index("dp")
    greet(groups, n + m - 2)
    firsts, seconds = [], []
    for k, (source, near, part, far) in enumerate(jobs):
        start, wait = copies(
            "dp", n, source, near, lambda peer, k=k: send_a.at[k, peer], lambda slot, k=k: recv_a.at[k, slot]
        )
        start()
        firsts.append(wait)
    for k, (source, near, part, far) in enumerate(jobs):
        firsts[k]()
        total = source(me)[...].astype(F32)
        for step in range(1, n):
            total = total + near(lax.rem(me + step, n))[...].astype(F32)
        part[...] = total.astype(BF16)
        start, wait = copies(
            "tensor",
            m,
            lambda peer, part=part: part,
            far,
            lambda peer, k=k: send_b.at[k, peer],
            lambda slot, k=k: recv_b.at[k, slot],
        )
        start()
        far(lax.axis_index("tensor"))[...] = part[...]
        seconds.append(wait)
    for wait in seconds:
        wait()


def job_semaphores(groups, jobs):
    n, m = groups["dp"], groups["tensor"]
    return [pltpu.SemaphoreType.DMA((jobs, n))] * 2 + [pltpu.SemaphoreType.DMA((jobs, m))] * 2


OWNER_PIECES = 4


def owner_kernel(groups, value, out, near, far, part, *semaphores):
    rows = out.shape[0] // OWNER_PIECES
    jobs = []
    for k in range(OWNER_PIECES):
        piece = pl.ds(k * rows, rows)
        jobs.append(
            (
                lambda peer, piece=piece: value.at[peer, piece, :],
                lambda slot, piece=piece: near.at[slot, piece, :],
                part.at[piece, :],
                lambda slot, piece=piece: far.at[slot, piece, :],
            )
        )
    run_jobs(groups, jobs, *semaphores)
    total = far[0].astype(F32)
    for slot in range(1, groups["tensor"]):
        total = total + far[slot].astype(F32)
    out[...] = total


def owner_total(value, groups, ident):
    n, m = groups["dp"], groups["tensor"]
    own = value.shape[1:]
    return pl.pallas_call(
        functools.partial(owner_kernel, groups),
        name="owner_total",
        in_specs=[pl.BlockSpec(memory_space=pltpu.VMEM)],
        out_specs=pl.BlockSpec(memory_space=pltpu.VMEM),
        out_shape=jax.ShapeDtypeStruct(own, F32),
        scratch_shapes=[
            pltpu.VMEM((n,) + own, BF16),
            pltpu.VMEM((m,) + own, BF16),
            pltpu.VMEM(own, BF16),
        ]
        + job_semaphores(groups, OWNER_PIECES),
        compiler_params=pltpu.CompilerParams(collective_id=ident, has_side_effects=True),
    )(value)


def head_kernel(groups, wide, narrow, wide_out, narrow_out, wide_near, narrow_near, wide_part, narrow_part, *semaphores):
    mine = lax.axis_index("tensor")
    jobs = [
        (
            lambda peer: narrow.at[peer, mine],
            lambda slot: narrow_near.at[slot],
            narrow_part,
            lambda slot: narrow_out.at[slot],
        )
    ]
    for k in range(wide.shape[2] // LANES):
        piece = pl.ds(k * LANES, LANES)
        jobs.append(
            (
                lambda peer, piece=piece: wide.at[peer, :, piece],
                lambda slot, piece=piece: wide_near.at[slot, :, piece],
                wide_part.at[:, piece],
                lambda slot, piece=piece: wide_out.at[slot, :, piece],
            )
        )
    run_jobs(groups, jobs, *semaphores)


def head_totals(wide, narrow, groups, ident):
    n, m = groups["dp"], groups["tensor"]
    wide_own, narrow_own = wide.shape[1:], narrow.shape[2:]
    return pl.pallas_call(
        functools.partial(head_kernel, groups),
        name="head_totals",
        in_specs=[pl.BlockSpec(memory_space=pltpu.VMEM)] * 2,
        out_specs=[pl.BlockSpec(memory_space=pltpu.VMEM)] * 2,
        out_shape=[jax.ShapeDtypeStruct((m,) + wide_own, BF16), jax.ShapeDtypeStruct((m,) + narrow_own, BF16)],
        scratch_shapes=[
            pltpu.VMEM((n,) + wide_own, BF16),
            pltpu.VMEM((n,) + narrow_own, BF16),
            pltpu.VMEM(wide_own, BF16),
            pltpu.VMEM(narrow_own, BF16),
        ]
        + job_semaphores(groups, 1 + wide.shape[2] // LANES),
        compiler_params=pltpu.CompilerParams(collective_id=ident, has_side_effects=True),
    )(wide, narrow)


def head_forward(rows, w_in_all, w_out_all):
    pre = jnp.dot(rows, w_in_all, preferred_element_type=F32)
    act, slope = gelu_parts(pre)
    hidden = act.astype(BF16)
    feats = jnp.dot(hidden, w_out_all, preferred_element_type=F32)
    unit, inv = unit_rows(feats)
    return (hidden, slope, unit, inv, unit.astype(BF16))


def head_backward(rows, hidden, slope, unit, inv, grad_unit, w_in_all, w_out_all):
    inner = jnp.sum(unit * grad_unit, axis=1, keepdims=True)
    grad_feats = (inv * (grad_unit - unit * inner)).astype(BF16)
    grad_out_part = lax.dot_general(
        hidden, grad_feats, (((0,), (0,)), ((), ())), preferred_element_type=F32
    )
    grad_hidden = lax.dot_general(
        grad_feats, w_out_all, (((1,), (1,)), ((), ())), preferred_element_type=F32
    )
    grad_pre = (grad_hidden * slope).astype(BF16)
    width = grad_pre.shape[1] // lax.axis_size("tensor")
    own_pre = lax.dynamic_slice_in_dim(grad_pre, lax.axis_index("tensor") * width, width, axis=1)
    grad_in_part = lax.dot_general(
        rows, own_pre, (((0,), (0,)), ((), ())), preferred_element_type=F32
    )
    grad_rows = lax.dot_general(
        grad_pre, w_in_all, (((1,), (1,)), ((), ())), preferred_element_type=F32
    )
    return (grad_in_part, grad_out_part, grad_rows)


def selection(masks):
    crops, patches = masks.shape
    size = crops * patches
    flat = masks.reshape(1, size)
    before = (
        lax.broadcasted_iota(jnp.int32, (size, size), 0) < lax.broadcasted_iota(jnp.int32, (size, size), 1)
    ).astype(BF16)
    place = jnp.dot(flat.astype(BF16), before, preferred_element_type=F32).astype(jnp.int32)
    slots = lax.broadcasted_iota(jnp.int32, (CAP, size), 0)
    picked = (place == slots) & (flat > 0)
    dead = slots >= jnp.sum(flat)
    first = lax.broadcasted_iota(jnp.int32, (CAP, size), 1) == 0
    return (picked | (dead & first)).astype(BF16), picked.astype(BF16)


def shards(groups, tokens, teacher_feats, masks, w_in, w_out, proto_student, proto_teacher):
    pick, place = selection(masks)
    counts = jnp.sum(masks, axis=1)
    ends = jnp.sum(
        jnp.where(jnp.arange(counts.shape[0])[:, None] <= jnp.arange(counts.shape[0])[None, :], counts[:, None], 0),
        axis=0,
    )
    slot = jnp.arange(CAP)[:, None]
    member = ((slot >= (ends - counts)[None, :]) & (slot < ends[None, :])).astype(F32)
    inverse = 1.0 / jnp.maximum(counts, 1).astype(F32)
    weight = (GRAD_SCALE * jnp.sum(member * inverse[None, :], axis=1)).astype(BF16)
    teacher_pick = jnp.dot(pick, teacher_feats, preferred_element_type=F32)
    teacher_rows = unit_rows(teacher_pick)[0].astype(BF16)
    teacher_every, weight_every = gather_rows((teacher_rows, weight.astype(F32).reshape(-1, LANES)), groups, 6)
    teacher_every, w_in, w_out = lax.optimization_barrier((teacher_every, w_in, w_out))
    w_in_all = lax.all_gather(w_in, "dp", axis=0, tiled=True)
    w_out_all = lax.all_gather(w_out, "dp", axis=0, tiled=True)
    teacher_every = teacher_every.reshape(-1, teacher_rows.shape[1])
    weight_every = weight_every.reshape(-1, LANES)
    live_every = (weight_every > 0).astype(F32)

    expo, row_sum = prototype_first(teacher_every, proto_teacher, live_every)
    row_sum = everywhere_total(row_sum, groups, 1)

    for turn in range(ROUNDS - 2):
        row_sum = prototype_middle(expo, live_every, row_sum)
        row_sum = everywhere_total(row_sum, groups, 2 + turn)

    rows = jnp.dot(pick, tokens, preferred_element_type=F32).astype(BF16)
    rows, row_sum = lax.optimization_barrier((rows, row_sum))
    hidden, slope, unit, inv, student_rows = head_forward(rows, w_in_all, w_out_all)
    (student_every,) = gather_rows((student_rows,), groups, 7)
    student_every = student_every.reshape(-1, student_rows.shape[1])

    raised, v, sums = prototype_last(expo, live_every, row_sum, student_every, proto_student)
    sums = everywhere_total(sums, groups, ROUNDS)
    grad_part, grad_proto = prototype_grad(
        expo, raised, v, live_every, weight_every, sums, student_every.T, proto_student
    )
    grad_unit = owner_total(grad_part.reshape(groups["dp"], CAP, -1), groups, ROUNDS + 1)

    dense = live_every.shape[0]
    own = CAP // LANES
    start = lax.axis_index("dp") * own

    def mine(values):
        return lax.dynamic_slice_in_dim(values, start, own).reshape(CAP)

    live_own = mine(live_every)
    scale_row = live_own / (mine(sums[:dense]) + 1.0 - live_own)
    row_loss = jnp.log(mine(sums[dense : 2 * dense])) - scale_row * mine(sums[2 * dense :])
    crop_loss = jnp.sum(member * row_loss[:, None], axis=0) * inverse

    grad_in_part, grad_out_part, grad_rows = head_backward(
        rows, hidden, slope, unit, inv, grad_unit, w_in_all, w_out_all
    )
    n, m = groups["dp"], groups["tensor"]
    wide = grad_in_part.astype(BF16).reshape(n, -1, grad_in_part.shape[1])
    narrow = grad_out_part.astype(BF16).reshape(n, m, -1, grad_out_part.shape[1])
    wide, narrow = head_totals(wide, narrow, groups, ROUNDS + 5)
    grad_in = wide.transpose(1, 0, 2).reshape(wide.shape[1], -1).astype(F32)
    grad_out = narrow.reshape(-1, narrow.shape[2]).astype(F32)
    d_tokens = lax.dot_general(
        place, grad_rows.astype(BF16), (((0,), (0,)), ((), ())), preferred_element_type=F32
    ).astype(BF16)
    return (d_tokens, grad_in, grad_out, grad_proto, crop_loss)


def solution(mesh):
    groups = {"dp": mesh.shape["dp"], "tensor": mesh.shape["tensor"]}
    placed = (
        P("dp", None),
        P("dp", None),
        P("dp", None),
        P("dp", None),
        P("dp", None),
        P(None, ("dp", "tensor")),
        P(None, ("dp", "tensor")),
    )
    return jax.shard_map(
        functools.partial(shards, groups),
        mesh=mesh,
        in_specs=placed,
        out_specs=(P("dp", None), P("dp", None), P("dp", None), P(None, ("dp", "tensor")), P("dp")),
        check_vma=False,
    )
```
